32 devices in a mesh: bead: 16 (over z, y, x), space: 2 (over core).
Axes of the slice: x: 2, y: 2, z: 4, core: 2. Of those that a mesh axis runs over, the one named last changes fastest.
Arguments:
- positions: float32 [32, 3, 16384], P('bead', None, 'space'), may hold values from -6 to 6
- momenta: float32 [32, 3, 16384], P('bead', None, 'space'), may hold values from -6 to 6
- forces: float32 [32, 3, 16384], P('bead', None, 'space'), may hold values from -6 to 6
- gle_drift: float32 [32, 5, 5], replicated, may hold values from -0.25 to 0.98, as said below
- gle_noise_mix: float32 [32, 5, 5], replicated, may hold values from -1.5 to 1.5
- aux_momenta: float32 [32, 4, 3, 16384], P(None, None, None, ('space', 'bead')), may hold values from -6 to 6
- noise: float32 [2, 32, 5, 3, 16384], P(None, None, None, None, ('space', 'bead')), may hold values from -6 to 6
Outputs:
- positions_out: float32 [32, 3, 16384], P('bead', None, 'space')
- momenta_out: float32 [32, 3, 16384], P('bead', None, 'space')
- forces_out: float32 [32, 3, 16384], P('bead', None, 'space')
- aux_out: float32 [32, 4, 3, 16384], P(None, None, None, ('space', 'bead'))
The draws below stay inside these ranges and needn't reach their ends.
Inputs may be any that keep to these rules, and one draw needn't show every extreme that they name: `gle_drift`: one matrix a mode; diagonal entries positive.
All inputs are finite; a program needn't handle non-finite values.
Results may differ from the reference program's by a relative error of at most 0.00012.
Values sent between devices are 32-bit elements; how exact they have to be, the bound alone decides.
No kernel may reach another device: no remote copies, remote signals or barrier semaphores. Data moves between devices by JAX's collectives and lax.ppermute only.
A program may use at most 64 MiB of HBM per device.

```python
import jax
import jax.numpy as jnp
from jax import lax

BEADS = 32
CELL_ATOMS = 128
AUX_MOMENTA = 4
STEPS = 2
DOMAIN_ATOMS = 8192
ATOMS = 16384
CELLS = 128
N_BEAD = 16
N_SPACE = 2


def draw_gle_drift(key, part):
    first, second = jax.random.split(jax.random.fold_in(key, 11))
    diagonal = jax.random.uniform(first, (BEADS, AUX_MOMENTA + 1), jnp.float32, 0.5, 0.95)
    outside = jax.random.uniform(second, (BEADS, AUX_MOMENTA + 1, AUX_MOMENTA + 1), jnp.float32, -0.25, 0.25)
    identity = jnp.eye(AUX_MOMENTA + 1, dtype=jnp.float32)[None]
    return outside * (1.0 - identity) + identity * diagonal[:, :, None]


def block_levels(own_key, dims, shards, least, top_value):
    loudness, own = 1.0, jax.random.fold_in(own_key, 6)
    for dim, shards_of in shards:
        draws = jnp.exp(jax.random.uniform(jax.random.fold_in(own, dim), (shards_of,), jnp.float32, least / len(shards), top_value / len(shards)))
        loudness = loudness * jnp.repeat(draws, dims[dim] // shards_of).reshape([-1 if axis == dim else 1 for axis in range(len(dims))])
    return loudness


def scatter_about(stream_key, shape, width, most, cuts=(), held_as=jnp.bfloat16):
    factor_of = block_levels(stream_key, shape, cuts, -0.22, 0.18) if cuts else 1.0
    values = jax.random.normal(stream_key, shape, jnp.float32) * width * factor_of
    return jnp.minimum(jnp.maximum(values, -most), most).astype(held_as)


def setup_inputs(seed: int = 0) -> dict:
    splits = jax.random.split(jax.random.key(seed), 8)
    positions = scatter_about(splits[0], (BEADS, 3, ATOMS), 1.0, 6.0, ((0, 16), (2, 2)), jnp.float32)
    momenta = scatter_about(splits[1], (BEADS, 3, ATOMS), 1.0, 6.0, ((0, 16), (2, 2)), jnp.float32)
    forces = scatter_about(splits[2], (BEADS, 3, ATOMS), 1.0, 6.0, ((0, 16), (2, 2)), jnp.float32)
    gle_drift = draw_gle_drift(jax.random.fold_in(splits[7], 71), 0)
    gle_noise_mix = scatter_about(splits[4], (BEADS, AUX_MOMENTA + 1, AUX_MOMENTA + 1), 0.3, 1.5, (), jnp.float32)
    aux_momenta = scatter_about(splits[5], (BEADS, AUX_MOMENTA, 3, ATOMS), 1.0, 6.0, ((3, 32),), jnp.float32)
    noise = scatter_about(splits[6], (STEPS, BEADS, AUX_MOMENTA + 1, 3, ATOMS), 1.0, 6.0, ((4, 32),), jnp.float32)
    return dict(positions=positions, momenta=momenta, forces=forces, gle_drift=gle_drift, gle_noise_mix=gle_noise_mix, aux_momenta=aux_momenta, noise=noise)


time_step = 0.5
cycle_freq = 1.5
cell_length = 2.0
pair_strength = 0.1
pair_range = 1.0

def mode_basis():
    index = jnp.arange(BEADS)
    bead_pos = index.astype(jnp.float32)[:, None]
    mode_pos = index.astype(jnp.float32)[None, :]
    phase = 2.0 * jnp.pi * bead_pos * mode_pos / BEADS
    kk = index[None, :]
    low = jnp.sqrt(1.0 / BEADS) + 0.0 * phase
    basis = jnp.where(kk == 0, low, jnp.where(kk < BEADS // 2, jnp.sqrt(2.0 / BEADS) * jnp.cos(phase), jnp.where(kk == BEADS // 2, jnp.sqrt(1.0 / BEADS) * jnp.cos(phase), jnp.sqrt(2.0 / BEADS) * jnp.sin(phase))))
    freq = 2.0 * cycle_freq * jnp.sin(jnp.pi * index.astype(jnp.float32) / BEADS)
    return (basis, freq, index)

def pull(center, other):
    sa = lax.optimization_barrier(jnp.sum(center * center, axis=0))
    sb = lax.optimization_barrier(jnp.sum(other * other, axis=0))
    cross = jnp.einsum('cni,cnj->nij', center, other, precision=lax.Precision.HIGHEST)
    dist = sa[:, :, None] + sb[:, None, :] - 2.0 * cross
    weight = jnp.exp(-dist / (2.0 * pair_range))
    rowsum = lax.optimization_barrier(jnp.sum(weight, axis=2))
    pulled = jnp.einsum('nij,cnj->cni', weight, other, precision=lax.Precision.HIGHEST)
    return pair_strength / pair_range * (center * rowsum[None] - pulled)

def bead_force(coords):
    cells = coords.reshape(3, CELLS, CELL_ATOMS)
    total = jnp.zeros_like(cells)
    for delta in (-1, 0, 1):
        other = jnp.roll(cells, -delta, axis=1)
        offset = jnp.asarray([delta * cell_length, 0.0, 0.0], dtype=cells.dtype).reshape(3, 1, 1)
        total = total + pull(cells, other + offset)
    return total.reshape(3, ATOMS)

def to_physical(values):
    lead = values.shape[:-1]
    share = DOMAIN_ATOMS // (2 * N_BEAD)
    grid = values.reshape(lead + (N_SPACE, N_BEAD, 2, share))
    return jnp.swapaxes(grid, -3, -2).reshape(lead + (ATOMS,))

def to_owner(values):
    lead = values.shape[:-1]
    share = DOMAIN_ATOMS // (2 * N_BEAD)
    grid = values.reshape(lead + (N_SPACE, 2, N_BEAD, share))
    return jnp.swapaxes(grid, -3, -2).reshape(lead + (ATOMS,))

def reference(positions, momenta, forces, gle_drift, gle_noise_mix, aux_momenta, noise):
    basis, freq, index = mode_basis()
    half = 0.5 * time_step
    aux = to_physical(aux_momenta)
    noise_phys = to_physical(noise)
    force = forces
    cosine = jnp.cos(time_step * freq)[:, None, None]
    safe = jnp.where(index == 0, 1.0, freq)
    sinc = jnp.where(index == 0, time_step, jnp.sin(time_step * freq) / safe)[:, None, None]
    wsin = (freq * jnp.sin(time_step * freq))[:, None, None]
    for step in range(STEPS):
        momenta = momenta + half * force
        qmode = jnp.einsum('jk,jcn->kcn', basis, positions, precision=lax.Precision.HIGHEST)
        pmode = jnp.einsum('jk,jcn->kcn', basis, momenta, precision=lax.Precision.HIGHEST)
        state = jnp.concatenate([pmode[:, None], aux], axis=1)
        state = jnp.einsum('kab,kbcn->kacn', gle_drift, state, precision=lax.Precision.HIGHEST) + jnp.einsum('kab,kbcn->kacn', gle_noise_mix, noise_phys[step], precision=lax.Precision.HIGHEST)
        pmode = state[:, 0]
        aux = state[:, 1:]
        qnext = qmode * cosine + sinc * pmode
        pmode = pmode * cosine - wsin * qmode
        positions = jnp.einsum('jk,kcn->jcn', basis, qnext, precision=lax.Precision.HIGHEST)
        momenta = jnp.einsum('jk,kcn->jcn', basis, pmode, precision=lax.Precision.HIGHEST)
        force = lax.map(bead_force, positions)
        momenta = momenta + half * force
    return (positions, momenta, force, to_owner(aux))
```

```python
import functools
import math

import jax
import jax.numpy as jnp
import ml_dtypes
import numpy as np
from jax import lax
from jax.experimental import pallas as pl
from jax.experimental.pallas import tpu as pltpu
from jax.sharding import PartitionSpec as P

CELL_ATOMS = 128
AUX = 4
STEPS = 2

time_step = 0.5
cycle_freq = 1.5
cell_length = 2.0
pair_strength = 0.1
pair_range = 1.0

LANES = 128
LOG2E = math.log2(math.e)
HIGHEST = lax.Precision.HIGHEST
VMEM_SPEC = pl.BlockSpec(memory_space=pltpu.VMEM)
SMEM_SPEC = pl.BlockSpec(memory_space=pltpu.SMEM)


def call(kernel, out_shape, in_specs=None, scratch_shapes=(), **kwargs):
    many = isinstance(out_shape, (list, tuple))
    return pl.pallas_call(
        kernel,
        out_shape=out_shape,
        in_specs=in_specs,
        out_specs=[VMEM_SPEC] * len(out_shape) if many else VMEM_SPEC,
        scratch_shapes=scratch_shapes,
        compiler_params=pltpu.CompilerParams(vmem_limit_bytes=56 * 1024 * 1024),
        **kwargs,
    )


def f32(*shape):
    return jax.ShapeDtypeStruct(shape, jnp.float32)


def mode_tables(beads):
    j = np.arange(beads, dtype=np.float64)[:, None]
    k = np.arange(beads)[None, :]
    phase = 2.0 * np.pi * j * k / beads
    basis = np.where(
        k == 0,
        np.sqrt(1.0 / beads),
        np.where(
            k < beads // 2,
            np.sqrt(2.0 / beads) * np.cos(phase),
            np.where(
                k == beads // 2, np.sqrt(1.0 / beads) * np.cos(phase), np.sqrt(2.0 / beads) * np.sin(phase)
            ),
        ),
    )
    freq = 2.0 * cycle_freq * np.sin(np.pi * np.arange(beads) / beads)
    cosine = np.cos(time_step * freq)
    safe = np.where(np.arange(beads) == 0, 1.0, freq)
    sinc = np.where(np.arange(beads) == 0, time_step, np.sin(time_step * freq) / safe)
    wsin = freq * np.sin(time_step * freq)
    turn = np.stack([cosine, sinc, wsin], axis=1)
    return basis.astype(np.float32), turn.astype(np.float32)


def split3(value):
    first = value.astype(jnp.bfloat16).astype(jnp.float32)
    rest = value - first
    second = rest.astype(jnp.bfloat16).astype(jnp.float32)
    third = rest - second
    return first, second, third


def run_force(coords):
    width = coords.shape[1]
    inner = width // CELL_ATOMS - 2
    row = lax.broadcasted_iota(jnp.int32, (8, width), 0)
    coords = jnp.where(row < 3, coords, 0.0)

    def half_square(x):
        return (0.5 * LOG2E / pair_range) * jnp.sum(x * x, axis=0, keepdims=True)

    left = jnp.where(row < 3, coords * (LOG2E / pair_range), 0.0)
    left = jnp.where(row == 3, -half_square(coords), left)
    left = jnp.where(row == 4, 1.0, left)
    a1, a2, a3 = split3(left)
    left = jnp.transpose(jnp.concatenate([a1, a1, a2, a2, a1, a3], axis=0)).astype(jnp.bfloat16)

    def right(shift):
        x = jnp.where(row == 0, coords + shift, coords)
        x = jnp.where(row == 4, -half_square(x), x)
        x = jnp.where(row == 3, 1.0, x)
        b1, b2, b3 = split3(x)
        return jnp.concatenate([b1, b2, b1, b2, b3, b1], axis=0).astype(jnp.bfloat16)

    rights = {delta: right(delta * cell_length) for delta in (-1, 0, 1)}

    def cell(array, number, axis):
        return lax.slice_in_dim(array, number * CELL_ATOMS, (number + 1) * CELL_ATOMS, axis=axis)

    forces = []
    for number in range(1, inner + 1):
        total = jnp.zeros((16, CELL_ATOMS), jnp.float32)
        for delta in (-1, 0, 1):
            power = jnp.dot(
                cell(left, number + delta, 0),
                cell(rights[-delta], number, 1),
                preferred_element_type=jnp.float32,
            )
            weight = jnp.exp2(power)
            high = weight.astype(jnp.bfloat16)
            low = (weight - high.astype(jnp.float32)).astype(jnp.bfloat16)
            rows = cell(rights[delta], number + delta, 1)[:16]
            total = total + jnp.dot(rows, high, preferred_element_type=jnp.float32)
            total = total + jnp.dot(rows, low, preferred_element_type=jnp.float32)
        total = total[:8] + total[8:]
        center = cell(coords, number, 1)
        forces.append(
            (pair_strength / pair_range) * (center * total[3:4] - total)
        )
    return jnp.concatenate(forces, axis=1)


def send_kernel(q_ref, p_ref, f_ref, out_ref, *, groups, span):
    beads_here = q_ref.shape[0]
    half = q_ref.shape[2] // 2
    rows = beads_here * 2 * span * 3
    quarter = 0.5 * time_step

    def one(b, carry):
        for j in range(beads_here):
            for h in range(2):
                for u in range(span):
                    at = pl.multiple_of(h * half + (b * span + u) * LANES, LANES)
                    place = ((j * 2 + h) * span + u) * 3
                    lanes = pl.ds(at, LANES)
                    out_ref[pl.ds(b * 2 * rows + place, 3), :] = q_ref[j, :, lanes]
                    out_ref[pl.ds(b * 2 * rows + rows + place, 3), :] = (
                        p_ref[j, :, lanes] + quarter * f_ref[j, :, lanes]
                    )
        return carry

    lax.fori_loop(0, groups, one, 0)


def noise_kernel(drift_ref, mix_ref, aux_ref, noise_ref, first_ref, second_ref):
    beads = aux_ref.shape[0]
    size = AUX + 1
    tiles = aux_ref.shape[3] // LANES

    def one(k, carry):
        base = k * size * size
        noises = [noise_ref[0, k, b] for b in range(size)]
        others = [aux_ref[k, b] for b in range(AUX)]
        for a in range(size):
            total = mix_ref[base + a * size] * noises[0]
            for b in range(1, size):
                total = total + mix_ref[base + a * size + b] * noises[b]
            for b in range(AUX):
                total = total + drift_ref[base + a * size + b + 1] * others[b]
            for t in range(tiles):
                first_ref[a, t, pl.ds(k * 3, 3), :] = total[:, t * LANES : (t + 1) * LANES]
        noises = [noise_ref[1, k, b] for b in range(size)]
        for a in range(size):
            total = mix_ref[base + a * size] * noises[0]
            for b in range(1, size):
                total = total + mix_ref[base + a * size + b] * noises[b]
            for t in range(tiles):
                second_ref[a, t, pl.ds(k * 3, 3), :] = total[:, t * LANES : (t + 1) * LANES]
        return carry

    lax.fori_loop(0, beads, one, 0)


def strided(ref, start, size, stride):
    return ref[pl.ds(start, size, stride=stride), :]


def turned(qm, p0, turn):
    cosine, sinc, wsin = turn[:, 0:1], turn[:, 1:2], turn[:, 2:3]
    return qm * cosine + sinc * p0, p0 * cosine - wsin * qm


def first_kernel(
    flag_ref, got_ref, pre_ref, gather_ref, basis_ref, turn_ref, drift_ref,
    own_ref, up0_ref, up1_ref, dn0_ref, dn1_ref, qn_ref, pn_ref, aux_ref, *, groups, span,
):
    beads = basis_ref.shape[0]
    beads_here = beads // groups
    rows = beads_here * 2 * span * 3
    places = [(h, u, c) for h in range(2) for u in range(span) for c in range(3)]

    def gathered(which):
        columns = []
        for h, u, c in places:
            parts = [
                strided(got_ref, which * rows + ((j * 2 + h) * span + u) * 3 + c, groups, 2 * rows)
                for j in range(beads_here)
            ]
            columns.append(jnp.concatenate(parts, axis=0))
        return jnp.concatenate(columns, axis=1)

    gather = gather_ref[...]
    qm = jnp.dot(gather, gathered(0), precision=HIGHEST, preferred_element_type=jnp.float32)
    pm = jnp.dot(gather, gathered(1), precision=HIGHEST, preferred_element_type=jnp.float32)

    def pre(a):
        return jnp.concatenate(
            [strided(pre_ref.at[a, h * span + u], c, beads, 3) for h, u, c in places], axis=1
        )

    drift = drift_ref[...]
    p0 = drift[:, 0:1] * pm + pre(0)
    for a in range(1, AUX + 1):
        aux_ref[a - 1] = drift[:, a * (AUX + 1) : a * (AUX + 1) + 1] * pm + pre(a)
    qn, pn = turned(qm, p0, turn_ref[...])
    qn_ref[...] = qn
    pn_ref[...] = pn
    new = jnp.dot(basis_ref[...], qn, precision=HIGHEST, preferred_element_type=jnp.float32)
    own_ref[...] = jnp.zeros_like(own_ref)
    value = {}
    for number, (h, u, c) in enumerate(places):
        value[h, u, c] = new[:, number * LANES : (number + 1) * LANES]
        own_ref[h, u, pl.ds(c, beads, stride=8), :] = value[h, u, c]
    top = flag_ref[0] == groups - 1
    bottom = flag_ref[0] == 0
    for c in range(3):
        here = pl.ds(c * beads, beads)
        last0, last1 = value[0, span - 1, c], value[1, span - 1, c]
        up0_ref[here, :] = jnp.where(top, last1, last0)
        up1_ref[here, :] = jnp.where(top, last0, last1)
        dn0_ref[here, :] = jnp.where(bottom, value[1, 0, c], value[0, 0, c])
        dn1_ref[here, :] = jnp.where(bottom, value[0, 0, c], value[1, 0, c])


def second_kernel(
    own_ref, up0_ref, up1_ref, dn0_ref, dn1_ref, qn_ref, pn_ref, aux_ref, pre_ref,
    spread_ref, basis_ref, turn_ref, drift_ref,
    sendq_ref, sendp_ref, auxout_ref, halo_ref, force_ref, *, span,
):
    beads = basis_ref.shape[0]
    places = [(h, u, c) for h in range(2) for u in range(span) for c in range(3)]
    halo_ref[...] = jnp.zeros_like(halo_ref)
    for number, ref in enumerate((up0_ref, up1_ref, dn0_ref, dn1_ref)):
        for c in range(3):
            halo_ref[number, pl.ds(c, beads, stride=8), :] = ref[pl.ds(c * beads, beads), :]

    def one(bead, carry):
        here = pl.ds(pl.multiple_of(bead * 8, 8), 8)
        for h in range(2):
            coords = jnp.concatenate(
                [halo_ref[h, here, :]]
                + [own_ref[h, u, here, :] for u in range(span)]
                + [halo_ref[2 + h, here, :]],
                axis=1,
            )
            force = run_force(coords)
            for u in range(span):
                force_ref[h, u, here, :] = force[:, u * LANES : (u + 1) * LANES]
        return carry

    lax.fori_loop(0, beads, one, 0)

    force = jnp.concatenate([strided(force_ref.at[h, u], c, beads, 8) for h, u, c in places], axis=1)
    fm = jnp.dot(spread_ref[...], force, precision=HIGHEST, preferred_element_type=jnp.float32)
    pm = pn_ref[...] + time_step * fm
    drift = drift_ref[...]
    state = [pm] + [aux_ref[a] for a in range(AUX)]
    news = []
    for a in range(AUX + 1):
        total = jnp.concatenate(
            [strided(pre_ref.at[a, h * span + u], c, beads, 3) for h, u, c in places], axis=1
        )
        for b in range(AUX + 1):
            number = a * (AUX + 1) + b
            total = total + drift[:, number : number + 1] * state[b]
        news.append(total)
    for a in range(AUX):
        auxout_ref[a] = news[a + 1]
    qn, pn = turned(qn_ref[...], news[0], turn_ref[...])
    basis = basis_ref[...]
    newq = jnp.dot(basis, qn, precision=HIGHEST, preferred_element_type=jnp.float32)
    newp = jnp.dot(basis, pn, precision=HIGHEST, preferred_element_type=jnp.float32)
    for number in range(len(places)):
        lanes = slice(number * LANES, (number + 1) * LANES)
        sendq_ref[pl.ds(number, beads, stride=len(places)), :] = newq[:, lanes]
        sendp_ref[pl.ds(number, beads, stride=len(places)), :] = newp[:, lanes]


def aux_kernel(aux_ref, out_ref, rows_ref):
    beads = aux_ref.shape[1]
    tiles = out_ref.shape[3] // LANES
    for a in range(AUX):
        for t in range(tiles):
            for c in range(3):
                number = t * 3 + c
                rows_ref[a * tiles + t, pl.ds(c, beads, stride=3), :] = aux_ref[
                    a, :, number * LANES : (number + 1) * LANES
                ]

    def one(k, carry):
        for a in range(AUX):
            for t in range(tiles):
                out_ref[k, a, :, t * LANES : (t + 1) * LANES] = rows_ref[a * tiles + t, pl.ds(k * 3, 3), :]
        return carry

    lax.fori_loop(0, beads, one, 0)


def bead_kernel(got_ref, before_ref, after_ref, q_ref, f_ref, x_ref, *, groups, span, block):
    beads_here = q_ref.shape[0]
    cells = q_ref.shape[2] // LANES
    x_ref[...] = jnp.zeros_like(x_ref)
    for j in range(beads_here):
        x_ref[j, 0:3, 0:LANES] = before_ref[j]
        x_ref[j, 0:3, (cells + 1) * LANES : (cells + 2) * LANES] = after_ref[j]

    def place(b, carry):
        for j in range(beads_here):
            for h in range(2):
                for u in range(span):
                    row = b * (beads_here * 2 * span * 3) + ((j * 2 + h) * span + u) * 3
                    cell = h * (cells // 2) + b * span + u
                    value = got_ref[pl.ds(row, 3), :]
                    q_ref[j, :, pl.ds(pl.multiple_of(cell * LANES, LANES), LANES)] = value
                    x_ref[j, 0:3, pl.ds(pl.multiple_of((cell + 1) * LANES, LANES), LANES)] = value
        return carry

    lax.fori_loop(0, groups, place, 0)

    def one(number, carry):
        at = pl.multiple_of(number * block * LANES, LANES)
        for j in range(beads_here):
            force = run_force(x_ref[j, :, pl.ds(at, (block + 2) * LANES)])
            f_ref[j, :, pl.ds(at, block * LANES)] = force[0:3]
        return carry

    lax.fori_loop(0, cells // block, one, 0)


def last_kernel(got_ref, f_ref, out_ref, *, groups, span):
    beads_here = f_ref.shape[0]
    cells = f_ref.shape[2] // LANES
    half = 0.5 * time_step

    def place(b, carry):
        for j in range(beads_here):
            for h in range(2):
                for u in range(span):
                    row = b * (beads_here * 2 * span * 3) + ((j * 2 + h) * span + u) * 3
                    cell = h * (cells // 2) + b * span + u
                    lanes = pl.ds(pl.multiple_of(cell * LANES, LANES), LANES)
                    out_ref[j, :, lanes] = got_ref[pl.ds(row, 3), :] + half * f_ref[j, :, lanes]
        return carry

    lax.fori_loop(0, groups, place, 0)


def on_device(positions, momenta, forces, gle_drift, gle_noise_mix, aux_momenta, noise):
    beads_here, _, atoms_here = positions.shape
    beads = gle_drift.shape[0]
    groups = lax.axis_size("bead")
    spaces = lax.axis_size("space")
    share = atoms_here // (2 * groups)
    span = share // CELL_ATOMS
    cells = atoms_here // CELL_ATOMS
    columns = 2 * span * 3
    width = columns * LANES
    size = AUX + 1
    basis, turn = mode_tables(beads)
    order = np.array([b * beads_here + j for j in range(beads_here) for b in range(groups)])
    gather = jnp.asarray(np.ascontiguousarray(basis[order].T))
    spread = jnp.asarray(np.ascontiguousarray(basis.T))
    basis = jnp.asarray(basis)
    turn = jnp.asarray(turn)
    drift_rows = gle_drift.reshape(beads, size * size)
    me = lax.axis_index("bead").astype(jnp.int32).reshape(1)

    def exchanged(block):
        return lax.all_to_all(block, "bead", split_axis=0, concat_axis=0, tiled=True)

    send = call(
        functools.partial(send_kernel, groups=groups, span=span),
        f32(groups * 2 * beads_here * columns, LANES),
        [VMEM_SPEC] * 3,
    )(positions, momenta, forces)
    got = exchanged(send)
    first, second = call(
        noise_kernel,
        [f32(size, 2 * span, beads * 3, LANES)] * 2,
        [SMEM_SPEC, SMEM_SPEC, VMEM_SPEC, VMEM_SPEC],
    )(gle_drift.reshape(-1), gle_noise_mix.reshape(-1), aux_momenta, noise)

    halo = f32(beads * 3, LANES)
    own, up0, up1, dn0, dn1, qn, pn, aux = call(
        functools.partial(first_kernel, groups=groups, span=span),
        [f32(2, span, beads * 8, LANES), halo, halo, halo, halo, f32(beads, width), f32(beads, width),
         f32(AUX, beads, width)],
        [SMEM_SPEC] + [VMEM_SPEC] * 6,
    )(me, got, first, gather, basis, turn, drift_rows)

    def shifted(block, step, wrap):
        route = []
        for b in range(groups):
            for s in range(spaces):
                to_b, to_s = b + step, s
                if not 0 <= to_b < groups:
                    to_b, to_s = to_b % groups, (s + wrap) % spaces
                route.append((b * spaces + s, to_b * spaces + to_s))
        return lax.ppermute(block, ("bead", "space"), route)

    up0 = shifted(up0, 1, 1)
    up1 = shifted(up1, 1, 0)
    dn0 = shifted(dn0, -1, 0)
    dn1 = shifted(dn1, -1, -1)

    rows = beads * columns
    sendq, sendp, aux = call(
        functools.partial(second_kernel, span=span),
        [f32(rows, LANES), f32(rows, LANES), f32(AUX, beads, width)],
        [VMEM_SPEC] * 13,
        scratch_shapes=[
            pltpu.VMEM((4, beads * 8, LANES), jnp.float32),
            pltpu.VMEM((2, span, beads * 8, LANES), jnp.float32),
        ],
    )(own, up0, up1, dn0, dn1, qn, pn, aux, second, spread, basis, turn, drift_rows)
    gotq = exchanged(sendq)
    gotp = exchanged(sendp)
    aux_out = call(
        aux_kernel,
        f32(*aux_momenta.shape),
        [VMEM_SPEC],
        scratch_shapes=[pltpu.VMEM((AUX * 2 * span, beads * 3, LANES), jnp.float32)],
    )(aux)

    per_owner = gotq.reshape(groups, beads_here, 2 * span, 3, LANES)
    head = per_owner[0, :, 0]
    tail = per_owner[groups - 1, :, 2 * span - 1]
    before = lax.ppermute(tail, "space", [(s, (s + 1) % spaces) for s in range(spaces)])
    after = lax.ppermute(head, "space", [(s, (s - 1) % spaces) for s in range(spaces)])
    block = math.gcd(cells, 8)
    positions_out, forces_out = call(
        functools.partial(bead_kernel, groups=groups, span=span, block=block),
        [f32(*positions.shape)] * 2,
        [VMEM_SPEC] * 3,
        scratch_shapes=[pltpu.VMEM((beads_here, 8, (cells + 2) * LANES), jnp.float32)],
    )(gotq, before, after)
    momenta_out = call(
        functools.partial(last_kernel, groups=groups, span=span),
        f32(*momenta.shape),
        [VMEM_SPEC] * 2,
    )(gotp, forces_out)
    return positions_out, momenta_out, forces_out, aux_out


def solution(mesh):
    in_specs = (
        P("bead", None, "space"),
        P("bead", None, "space"),
        P("bead", None, "space"),
        P(),
        P(),
        P(None, None, None, ("space", "bead")),
        P(None, None, None, None, ("space", "bead")),
    )
    out_specs = (
        P("bead", None, "space"),
        P("bead", None, "space"),
        P("bead", None, "space"),
        P(None, None, None, ("space", "bead")),
    )
    return jax.shard_map(
        on_device, mesh=mesh, in_specs=in_specs, out_specs=out_specs, check_vma=False
    )
```

```python
import functools
import math

import jax
import jax.numpy as jnp
import ml_dtypes
import numpy as np
from jax import lax
from jax.experimental import pallas as pl
from jax.experimental.pallas import tpu as pltpu
from jax.sharding import PartitionSpec as P

CELL_ATOMS = 128
AUX = 4
STEPS = 2

time_step = 0.5
cycle_freq = 1.5
cell_length = 2.0
pair_strength = 0.1
pair_range = 1.0

LANES = 128
LOG2E = math.log2(math.e)
HIGHEST = lax.Precision.HIGHEST
VMEM_SPEC = pl.BlockSpec(memory_space=pltpu.VMEM)
SMEM_SPEC = pl.BlockSpec(memory_space=pltpu.SMEM)


def call(kernel, out_shape, in_specs=None, scratch_shapes=(), **kwargs):
    many = isinstance(out_shape, (list, tuple))
    return pl.pallas_call(
        kernel,
        out_shape=out_shape,
        in_specs=in_specs,
        out_specs=[VMEM_SPEC] * len(out_shape) if many else VMEM_SPEC,
        scratch_shapes=scratch_shapes,
        compiler_params=pltpu.CompilerParams(vmem_limit_bytes=56 * 1024 * 1024),
        **kwargs,
    )


def f32(*shape):
    return jax.ShapeDtypeStruct(shape, jnp.float32)


def mode_tables(beads):
    j = np.arange(beads, dtype=np.float64)[:, None]
    k = np.arange(beads)[None, :]
    phase = 2.0 * np.pi * j * k / beads
    basis = np.where(
        k == 0,
        np.sqrt(1.0 / beads),
        np.where(
            k < beads // 2,
            np.sqrt(2.0 / beads) * np.cos(phase),
            np.where(
                k == beads // 2, np.sqrt(1.0 / beads) * np.cos(phase), np.sqrt(2.0 / beads) * np.sin(phase)
            ),
        ),
    )
    freq = 2.0 * cycle_freq * np.sin(np.pi * np.arange(beads) / beads)
    cosine = np.cos(time_step * freq)
    safe = np.where(np.arange(beads) == 0, 1.0, freq)
    sinc = np.where(np.arange(beads) == 0, time_step, np.sin(time_step * freq) / safe)
    wsin = freq * np.sin(time_step * freq)
    turn = np.stack([cosine, sinc, wsin], axis=1)
    return basis.astype(np.float32), turn.astype(np.float32)


def split3(value):
    first = value.astype(jnp.bfloat16).astype(jnp.float32)
    rest = value - first
    second = rest.astype(jnp.bfloat16).astype(jnp.float32)
    third = rest - second
    return first, second, third


def prepare(coords, left_ref, right_ref, slot, want_left, shifts):
    row = lax.broadcasted_iota(jnp.int32, coords.shape, 0)

    def half_square(x):
        return (0.5 * LOG2E / pair_range) * jnp.sum(x * x, axis=0, keepdims=True)

    if want_left:
        x = jnp.where(row == 3, -half_square(coords), coords * (LOG2E / pair_range))
        x = jnp.where(row == 4, 1.0, x)
        a1, a2, a3 = split3(x)
        left = jnp.concatenate([a1, a1, a2, a2, a1, a3], axis=0)
        left_ref[slot] = jnp.transpose(left).astype(jnp.bfloat16)
    for delta in shifts:
        x = jnp.where(row == 0, coords + delta * cell_length, coords) if delta else coords
        x = jnp.where(row == 4, -half_square(x), x)
        x = jnp.where(row == 3, 1.0, x)
        b1, b2, b3 = split3(x)
        right_ref[slot, delta + 1] = jnp.concatenate([b1, b2, b1, b2, b3, b1], axis=0).astype(jnp.bfloat16)


def pair_scratch(slots, tiles):
    count = sum(len(of) for of in tiles)
    return [
        pltpu.VMEM((slots, CELL_ATOMS, 48), jnp.bfloat16),
        pltpu.VMEM((slots, 3, 48, CELL_ATOMS), jnp.bfloat16),
        pltpu.VMEM((count * CELL_ATOMS, CELL_ATOMS), jnp.float32),
        pltpu.VMEM((count * CELL_ATOMS, CELL_ATOMS), jnp.float32),
        pltpu.VMEM((2 * count * CELL_ATOMS, CELL_ATOMS), jnp.bfloat16),
        pltpu.VMEM((2 * count * CELL_ATOMS, CELL_ATOMS), jnp.bfloat16),
    ]


def pair_sums(steps, tiles, base_of, finish, left_ref, right_ref, e0_ref, e1_ref, w0_ref, w1_ref):
    n = CELL_ATOMS

    def powers(step, e_ref):
        base = base_of(step)
        at = 0
        for u, of in enumerate(tiles):
            for offset, delta in of:
                e_ref[at * n : (at + 1) * n] = jnp.dot(
                    left_ref[base + offset],
                    right_ref[base + 1 + u, 1 - delta],
                    preferred_element_type=jnp.float32,
                )
                at += 1

    def weights(e_ref, w_ref):
        at = 0
        for of in tiles:
            for number in range(len(of)):
                weight = jnp.exp2(e_ref[(at + number) * n : (at + number + 1) * n])
                high = weight.astype(jnp.bfloat16)
                low = (weight - high.astype(jnp.float32)).astype(jnp.bfloat16)
                place = 2 * at + number
                w_ref[place * n : (place + 1) * n] = high
                place += len(of)
                w_ref[place * n : (place + 1) * n] = low
            at += len(of)

    def sums(step, w_ref):
        base = base_of(step)
        at = 0
        for u, of in enumerate(tiles):
            if not of:
                continue
            rows = [right_ref[base + offset, delta + 1, 0:16] for offset, delta in of]
            total = jnp.dot(
                jnp.concatenate(rows + rows, axis=1),
                w_ref[2 * at * n : 2 * (at + len(of)) * n],
                preferred_element_type=jnp.float32,
            )
            finish(step, u, total[:8] + total[8:])
            at += len(of)

    def clamp(step):
        return jnp.clip(step, 0, steps - 1)

    def pair(i, carry):
        step = 2 * i
        sums(clamp(step - 2), w0_ref)
        weights(e1_ref, w1_ref)
        powers(clamp(step), e0_ref)
        sums(clamp(step - 1), w1_ref)
        weights(e0_ref, w0_ref)
        powers(clamp(step + 1), e1_ref)
        return carry

    lax.fori_loop(0, (steps + 3) // 2, pair, 0)


def place_loop(groups, span, one):
    def body(b, carry):
        for h in range(2):
            for u in range(span):
                cell = (h * groups + b) * span + u
                one(b, h * span + u, cell)
        return carry

    lax.fori_loop(0, groups, body, 0)


def lanes_of(cell):
    return pl.ds(pl.multiple_of(cell * LANES, LANES), LANES)


def send_kernel(q_ref, p_ref, f_ref, out_ref, *, groups, span):
    here = q_ref.shape[1]
    rows = here * 2 * span * 3
    quarter = 0.5 * time_step

    def one(b, tile, cell):
        lanes = lanes_of(cell)
        for c in range(3):
            row = b * 2 * rows + (tile * 3 + c) * here
            out_ref[pl.ds(row, here), :] = q_ref[c, :, lanes]
            out_ref[pl.ds(row + rows, here), :] = p_ref[c, :, lanes] + quarter * f_ref[c, :, lanes]

    place_loop(groups, span, one)


def columns_of(tiles):
    return [(t, c, slice((t * 3 + c) * LANES, (t * 3 + c + 1) * LANES)) for t in range(tiles) for c in range(3)]


def noise_kernel(drift_ref, mix_ref, aux_ref, noise_ref, first_ref, second_ref, rows_ref):
    beads = aux_ref.shape[0]
    size = AUX + 1
    tiles = aux_ref.shape[3] // LANES

    def copy(k, carry):
        for c in range(3):
            for t in range(tiles):
                rows_ref[c, t, pl.ds(k * AUX, AUX), :] = aux_ref[k, c, :, t * LANES : (t + 1) * LANES]
        return carry

    lax.fori_loop(0, beads, copy, 0)
    drift = drift_ref[...]
    mix = mix_ref[...]
    for t, c, lanes in columns_of(tiles):
        inner = slice(t * LANES, (t + 1) * LANES)
        others = [rows_ref[c, t, pl.ds(b, beads, stride=AUX), :] for b in range(AUX)]
        for s, ref in ((0, first_ref), (1, second_ref)):
            noises = [noise_ref[s, b, c, :, inner] for b in range(size)]
            for a in range(size):
                at = a * size
                total = mix[:, at : at + 1] * noises[0]
                for b in range(1, size):
                    total = total + mix[:, at + b : at + b + 1] * noises[b]
                if s == 0:
                    for b in range(AUX):
                        total = total + drift[:, at + b + 1 : at + b + 2] * others[b]
                ref[a, :, lanes] = total


def strided(ref, start, size, stride):
    return ref[pl.ds(start, size, stride=stride), :]


def turned(qm, p0, turn):
    cosine, sinc, wsin = turn[:, 0:1], turn[:, 1:2], turn[:, 2:3]
    return qm * cosine + sinc * p0, p0 * cosine - wsin * qm


def dot(a, b):
    return jnp.dot(a, b, precision=HIGHEST, preferred_element_type=jnp.float32)


def first_kernel(
    flag_ref, got_ref, pre_ref, gather_ref, basis_ref, turn_ref, drift_ref,
    own_ref, up0_ref, up1_ref, dn0_ref, dn1_ref, qn_ref, pn_ref, pm_ref, *, groups, span,
):
    beads = basis_ref.shape[0]
    here = beads // groups
    tiles = 2 * span
    rows = here * tiles * 3

    def gathered(which):
        columns = []
        for number in range(tiles * 3):
            parts = [
                strided(got_ref, which * rows + number * here + j, groups, 2 * rows) for j in range(here)
            ]
            columns.append(jnp.concatenate(parts, axis=0))
        return jnp.concatenate(columns, axis=1)

    gather = gather_ref[...]
    qm = dot(gather, gathered(0))
    pm = dot(gather, gathered(1))
    p0 = drift_ref[:, 0:1] * pm + pre_ref[0]
    qn, pn = turned(qm, p0, turn_ref[...])
    new = dot(basis_ref[...], qn)
    own_ref[...] = jnp.zeros_like(own_ref)
    value = {}
    for t, c, lanes in columns_of(tiles):
        value[t // span, t % span, c] = new[:, lanes]
        own_ref[t // span, t % span, pl.ds(c, beads, stride=8), :] = new[:, lanes]
    top = flag_ref[0] == groups - 1
    bottom = flag_ref[0] == 0
    for c in range(3):
        part = pl.ds(c * beads, beads)
        last0, last1 = value[0, span - 1, c], value[1, span - 1, c]
        up0_ref[part, :] = jnp.where(top, last1, last0)
        up1_ref[part, :] = jnp.where(top, last0, last1)
        dn0_ref[part, :] = jnp.where(bottom, value[1, 0, c], value[0, 0, c])
        dn1_ref[part, :] = jnp.where(bottom, value[0, 0, c], value[1, 0, c])
    qn_ref[...] = qn
    pn_ref[...] = pn
    pm_ref[...] = pm


def middle_kernel(pm_ref, first_ref, second_ref, drift_ref, out_ref):
    size = AUX + 1
    drift = drift_ref[...]
    for at in range(0, pm_ref.shape[1], LANES):
        lanes = slice(at, at + LANES)
        pm = pm_ref[:, lanes]
        aux = [drift[:, a * size : a * size + 1] * pm + first_ref[a, :, lanes] for a in range(1, size)]
        for a in range(size):
            total = second_ref[a, :, lanes]
            for b in range(AUX):
                total = total + drift[:, a * size + b + 1 : a * size + b + 2] * aux[b]
            out_ref[a, :, lanes] = total


def coefficient(center, sums):
    return (pair_strength / pair_range) * (center * sums[3:4] - sums)


def inner_kernel(own_ref, force_ref, *scratch, span, tiles):
    beads = own_ref.shape[2] // 8
    left_ref, right_ref = scratch[:2]

    def tile(bead):
        return pl.ds(pl.multiple_of(bead * 8, 8), 8)

    def one(bead, carry):
        for h in range(2):
            for u in range(span):
                prepare(
                    own_ref[h, u, tile(bead), :], left_ref, right_ref,
                    (2 * bead + h) * (span + 2) + u + 1, True, (-1, 0, 1),
                )
        return carry

    lax.fori_loop(0, beads, one, 0)

    def finish(step, u, sums):
        h, here = step % 2, tile(step // 2)
        force_ref[h, u, here, :] = coefficient(own_ref[h, u, here, :], sums)

    pair_sums(2 * beads, tiles, lambda step: step * (span + 2), finish, *scratch)


def outer_kernel(
    own_ref, part_ref, up0_ref, up1_ref, dn0_ref, dn1_ref, qn_ref, pn_ref, base_ref,
    gather_ref, basis_ref, turn_ref, drift_ref,
    sendq_ref, pm_ref, p0_ref, halo_ref, force_ref, *scratch, groups, span, tiles,
):
    beads = basis_ref.shape[0]
    here = beads // groups
    left_ref, right_ref = scratch[:2]
    halo_ref[...] = jnp.zeros_like(halo_ref)
    for number, ref in enumerate((up0_ref, up1_ref, dn0_ref, dn1_ref)):
        for c in range(3):
            halo_ref[number, pl.ds(c, beads, stride=8), :] = ref[pl.ds(c * beads, beads), :]

    def tile(bead):
        return pl.ds(pl.multiple_of(bead * 8, 8), 8)

    def one(bead, carry):
        at = tile(bead)
        for h in range(2):
            slot = (2 * bead + h) * (span + 2)
            prepare(halo_ref[h, at, :], left_ref, right_ref, slot, True, (-1,))
            prepare(halo_ref[2 + h, at, :], left_ref, right_ref, slot + span + 1, True, (1,))
            for u in sorted({0, span - 1}):
                shifts = tuple(sorted(-delta for _, delta in tiles[u]))
                prepare(own_ref[h, u, at, :], left_ref, right_ref, slot + u + 1, False, shifts)
        return carry

    lax.fori_loop(0, beads, one, 0)
    force_ref[...] = part_ref[...]

    def finish(step, u, sums):
        h, at = step % 2, tile(step // 2)
        force_ref[h, u, at, :] = part_ref[h, u, at, :] + coefficient(own_ref[h, u, at, :], sums)

    pair_sums(2 * beads, tiles, lambda step: step * (span + 2), finish, *scratch)

    force = jnp.concatenate(
        [strided(force_ref.at[t // span, t % span], c, beads, 8) for t, c, _ in columns_of(2 * span)], axis=1
    )
    pm = pn_ref[...] + time_step * dot(gather_ref[...], force)
    p0 = drift_ref[:, 0:1] * pm + base_ref[0]
    qn, _ = turned(qn_ref[...], p0, turn_ref[...])
    new = dot(basis_ref[...], qn)
    count = 6 * span
    for number in range(count):
        for j in range(here):
            sendq_ref[pl.ds(number * here + j, groups, stride=count * here), :] = new[
                j * groups : (j + 1) * groups, number * LANES : (number + 1) * LANES
            ]
    pm_ref[...] = pm
    p0_ref[...] = p0


def rest_kernel(
    pm_ref, p0_ref, qn_ref, base_ref, basis_ref, turn_ref, drift_ref,
    sendp_ref, out_ref, rows_ref, *, groups, span,
):
    beads = basis_ref.shape[0]
    here = beads // groups
    size = AUX + 1
    _, pn = turned(qn_ref[...], p0_ref[...], turn_ref[...])
    new = dot(basis_ref[...], pn)
    count = 6 * span
    for number in range(count):
        for j in range(here):
            sendp_ref[pl.ds(number * here + j, groups, stride=count * here), :] = new[
                j * groups : (j + 1) * groups, number * LANES : (number + 1) * LANES
            ]
    drift = drift_ref[...]
    for t, c, lanes in columns_of(2 * span):
        pm = pm_ref[:, lanes]
        for a in range(AUX):
            at = (a + 1) * size
            rows_ref[c, t, pl.ds(a, beads, stride=AUX), :] = drift[:, at : at + 1] * pm + base_ref[a + 1, :, lanes]

    def copy(k, carry):
        for c in range(3):
            for t in range(2 * span):
                out_ref[k, c, :, t * LANES : (t + 1) * LANES] = rows_ref[c, t, pl.ds(k * AUX, AUX), :]
        return carry

    lax.fori_loop(0, beads, copy, 0)


def bead_kernel(got_ref, before_ref, after_ref, q_ref, f_ref, x_ref, force_ref, *scratch, groups, span, block, tiles):
    here = q_ref.shape[1]
    cells = q_ref.shape[2] // LANES
    left_ref, right_ref = scratch[:2]
    x_ref[...] = jnp.zeros_like(x_ref)
    for j in range(here):
        x_ref[j * (cells + 2), 0:3] = strided(before_ref, j, 3, here)
        x_ref[(j + 1) * (cells + 2) - 1, 0:3] = strided(after_ref, j, 3, here)

    def place(b, tile, cell):
        row = (b * 2 * span + tile) * 3 * here
        for c in range(3):
            q_ref[c, :, lanes_of(cell)] = got_ref[pl.ds(row + c * here, here), :]
        for j in range(here):
            x_ref[j * (cells + 2) + cell + 1, 0:3] = got_ref[pl.ds(row + j, 3, stride=here), :]

    place_loop(groups, span, place)
    slots = here * (cells + 2)
    group = math.gcd(slots, 4)

    def one(number, carry):
        for k in range(group):
            slot = number * group + k
            prepare(x_ref[slot], left_ref, right_ref, slot, True, (-1, 0, 1))
        return carry

    lax.fori_loop(0, slots // group, one, 0)
    per_bead = cells // block

    def base_of(step):
        return (step // per_bead) * (cells + 2) + (step % per_bead) * block

    def finish(step, u, sums):
        at = pl.multiple_of((step * block + u) * 8, 8)
        force_ref[pl.ds(at, 8), :] = coefficient(x_ref[base_of(step) + 1 + u], sums)

    pair_sums(here * per_bead, tiles, base_of, finish, *scratch)

    def out(cell, carry):
        for c in range(3):
            f_ref[c, :, lanes_of(cell)] = strided(force_ref, cell * 8 + c, here, cells * 8)
        return carry

    lax.fori_loop(0, cells, out, 0)


def last_kernel(got_ref, f_ref, out_ref, *, groups, span):
    here = f_ref.shape[1]
    half = 0.5 * time_step

    def one(b, tile, cell):
        lanes = lanes_of(cell)
        row = (b * 2 * span + tile) * 3 * here
        for c in range(3):
            out_ref[c, :, lanes] = got_ref[pl.ds(row + c * here, here), :] + half * f_ref[c, :, lanes]

    place_loop(groups, span, one)


def on_device(positions, momenta, forces, gle_drift, gle_noise_mix, aux_momenta, noise):
    here, _, atoms_here = positions.shape
    beads = gle_drift.shape[0]
    groups = lax.axis_size("bead")
    spaces = lax.axis_size("space")
    span = atoms_here // (2 * groups * CELL_ATOMS)
    cells = atoms_here // CELL_ATOMS
    columns = 2 * span * 3
    width = columns * LANES
    size = AUX + 1
    basis, turn = mode_tables(beads)
    order = np.array([b * here + j for j in range(here) for b in range(groups)])
    gather = jnp.asarray(np.ascontiguousarray(basis[order].T))
    basis = jnp.asarray(np.ascontiguousarray(basis[order]))
    turn = jnp.asarray(turn)
    drift = gle_drift.reshape(beads, size * size)
    mix = gle_noise_mix.reshape(beads, size * size)
    me = lax.axis_index("bead").astype(jnp.int32).reshape(1)
    by_coord = functools.partial(jnp.transpose, axes=(1, 0, 2))
    grid = f32(3, here, atoms_here)

    def exchanged(block):
        return lax.all_to_all(block, "bead", split_axis=0, concat_axis=0, tiled=True)

    send = call(
        functools.partial(send_kernel, groups=groups, span=span),
        f32(groups * 2 * here * columns, LANES),
        [VMEM_SPEC] * 3,
    )(by_coord(positions), by_coord(momenta), by_coord(forces))
    got = exchanged(send)
    rows = pltpu.VMEM((3, 2 * span, beads * AUX, LANES), jnp.float32)
    first, second = call(
        noise_kernel,
        [f32(size, beads, width)] * 2,
        [VMEM_SPEC] * 4,
        scratch_shapes=[rows],
    )(drift, mix, jnp.transpose(aux_momenta, (0, 2, 1, 3)), jnp.transpose(noise, (0, 2, 3, 1, 4)))

    halo = f32(beads * 3, LANES)
    state = f32(beads, width)
    own, up0, up1, dn0, dn1, qn, pn, pm = call(
        functools.partial(first_kernel, groups=groups, span=span),
        [f32(2, span, beads * 8, LANES), halo, halo, halo, halo, state, state, state],
        [SMEM_SPEC] + [VMEM_SPEC] * 6,
    )(me, got, first, gather, basis, turn, drift)

    def shifted(block, step, wrap):
        route = []
        for b in range(groups):
            for s in range(spaces):
                to_b, to_s = b + step, s
                if not 0 <= to_b < groups:
                    to_b, to_s = to_b % groups, (s + wrap) % spaces
                route.append((b * spaces + s, to_b * spaces + to_s))
        return lax.ppermute(block, ("bead", "space"), route)

    up0 = shifted(up0, 1, 1)
    up1 = shifted(up1, 1, 0)
    dn0 = shifted(dn0, -1, 0)
    dn1 = shifted(dn1, -1, -1)

    slots = 2 * beads * (span + 2)
    inside = [
        [(v + 1, v - u) for v in range(span) if abs(v - u) <= 1] for u in range(span)
    ]
    outside = [
        ([(0, -1)] if u == 0 else []) + ([(span + 1, 1)] if u == span - 1 else []) for u in range(span)
    ]
    part = call(
        functools.partial(inner_kernel, span=span, tiles=inside),
        f32(2, span, beads * 8, LANES),
        [VMEM_SPEC],
        scratch_shapes=pair_scratch(slots, inside),
    )(own)
    base = call(middle_kernel, f32(size, beads, width), [VMEM_SPEC] * 4)(pm, first, second, drift)
    sendq, pm, p0 = call(
        functools.partial(outer_kernel, groups=groups, span=span, tiles=outside),
        [f32(beads * columns, LANES), state, state],
        [VMEM_SPEC] * 13,
        scratch_shapes=[
            pltpu.VMEM((4, beads * 8, LANES), jnp.float32),
            pltpu.VMEM((2, span, beads * 8, LANES), jnp.float32),
        ]
        + pair_scratch(slots, outside),
    )(own, part, up0, up1, dn0, dn1, qn, pn, base, gather, basis, turn, drift)
    gotq = exchanged(sendq)
    sendp, aux_out = call(
        functools.partial(rest_kernel, groups=groups, span=span),
        [f32(beads * columns, LANES), f32(beads, 3, AUX, aux_momenta.shape[3])],
        [VMEM_SPEC] * 7,
        scratch_shapes=[rows],
    )(pm, p0, qn, base, basis, turn, drift)
    gotp = exchanged(sendp)

    head = gotq[: 3 * here]
    tail = gotq[-3 * here :]
    before = lax.ppermute(tail, "space", [(s, (s + 1) % spaces) for s in range(spaces)])
    after = lax.ppermute(head, "space", [(s, (s - 1) % spaces) for s in range(spaces)])
    block = math.gcd(cells, 2)
    around = [[(u, -1), (u + 1, 0), (u + 2, 1)] for u in range(block)]
    new_q, new_f = call(
        functools.partial(bead_kernel, groups=groups, span=span, block=block, tiles=around),
        [grid] * 2,
        [VMEM_SPEC] * 3,
        scratch_shapes=[
            pltpu.VMEM((here * (cells + 2), 8, LANES), jnp.float32),
            pltpu.VMEM((here * cells * 8, LANES), jnp.float32),
        ]
        + pair_scratch(here * (cells + 2), around),
    )(gotq, before, after)
    new_p = call(
        functools.partial(last_kernel, groups=groups, span=span),
        grid,
        [VMEM_SPEC] * 2,
    )(gotp, new_f)
    return by_coord(new_q), by_coord(new_p), by_coord(new_f), jnp.transpose(aux_out, (0, 2, 1, 3))


def solution(mesh):
    in_specs = (
        P("bead", None, "space"),
        P("bead", None, "space"),
        P("bead", None, "space"),
        P(),
        P(),
        P(None, None, None, ("space", "bead")),
        P(None, None, None, None, ("space", "bead")),
    )
    out_specs = (
        P("bead", None, "space"),
        P("bead", None, "space"),
        P("bead", None, "space"),
        P(None, None, None, ("space", "bead")),
    )
    return jax.shard_map(
        on_device, mesh=mesh, in_specs=in_specs, out_specs=out_specs, check_vma=False
    )
```

```python
import functools
import math

import jax
import jax.numpy as jnp
import ml_dtypes
import numpy as np
from jax import lax
from jax.experimental import pallas as pl
from jax.experimental.pallas import tpu as pltpu
from jax.sharding import PartitionSpec as P

CELL_ATOMS = 128
AUX = 4
STEPS = 2

time_step = 0.5
cycle_freq = 1.5
cell_length = 2.0
pair_strength = 0.1
pair_range = 1.0

LANES = 128
LOG2E = math.log2(math.e)
HIGHEST = lax.Precision.HIGHEST
VMEM_SPEC = pl.BlockSpec(memory_space=pltpu.VMEM)
SMEM_SPEC = pl.BlockSpec(memory_space=pltpu.SMEM)


def call(kernel, out_shape, in_specs=None, scratch_shapes=(), **kwargs):
    many = isinstance(out_shape, (list, tuple))
    return pl.pallas_call(
        kernel,
        out_shape=out_shape,
        in_specs=in_specs,
        out_specs=[VMEM_SPEC] * len(out_shape) if many else VMEM_SPEC,
        scratch_shapes=scratch_shapes,
        compiler_params=pltpu.CompilerParams(vmem_limit_bytes=56 * 1024 * 1024),
        **kwargs,
    )


def f32(*shape):
    return jax.ShapeDtypeStruct(shape, jnp.float32)


def mode_tables(beads):
    j = np.arange(beads, dtype=np.float64)[:, None]
    k = np.arange(beads)[None, :]
    phase = 2.0 * np.pi * j * k / beads
    basis = np.where(
        k == 0,
        np.sqrt(1.0 / beads),
        np.where(
            k < beads // 2,
            np.sqrt(2.0 / beads) * np.cos(phase),
            np.where(
                k == beads // 2, np.sqrt(1.0 / beads) * np.cos(phase), np.sqrt(2.0 / beads) * np.sin(phase)
            ),
        ),
    )
    freq = 2.0 * cycle_freq * np.sin(np.pi * np.arange(beads) / beads)
    cosine = np.cos(time_step * freq)
    safe = np.where(np.arange(beads) == 0, 1.0, freq)
    sinc = np.where(np.arange(beads) == 0, time_step, np.sin(time_step * freq) / safe)
    wsin = freq * np.sin(time_step * freq)
    turn = np.stack([cosine, sinc, wsin], axis=1)
    return basis.astype(np.float32), turn.astype(np.float32)


def split3(value):
    first = value.astype(jnp.bfloat16).astype(jnp.float32)
    rest = value - first
    second = rest.astype(jnp.bfloat16).astype(jnp.float32)
    third = rest - second
    return first, second, third


def prepare(coords, left_ref, right_ref, slot, want_left, shifts):
    row = lax.broadcasted_iota(jnp.int32, coords.shape, 0)
    scale = LOG2E / pair_range
    square = (0.5 * scale) * jnp.sum(coords * coords, axis=0, keepdims=True)
    along = coords[0:1]
    if want_left:
        x = jnp.where(row > 3, 1.0, coords * scale)
        x = jnp.where(row == 3, -square, x)
        x = jnp.where(row == 7, along * scale, x)
        a1, a2, a3 = split3(x)
        left = jnp.concatenate([a1, a1, a2, a2, a1, a3], axis=0)
        left_ref[slot] = jnp.transpose(left).astype(jnp.bfloat16)
    shift = (row - 5).astype(jnp.float32) * cell_length
    x = jnp.where(row > 3, -square - scale * (shift * along + 0.5 * shift * shift), coords)
    x = jnp.where(row == 3, 1.0, x)
    b1, b2, b3 = split3(x)
    for delta in shifts:
        keep = (row <= 3) | (row == 5 + delta)
        c1 = jnp.where(keep, b1, jnp.where(row == 7, delta * cell_length, 0.0))
        c2 = jnp.where(keep, b2, 0.0)
        c3 = jnp.where(keep, b3, 0.0)
        right_ref[slot, delta + 1] = jnp.concatenate([c1, c2, c1, c2, c3, c1], axis=0).astype(jnp.bfloat16)


def pair_scratch(slots, units):
    count = sum(len(others) for _, _, others in units)
    return [
        pltpu.VMEM((slots, CELL_ATOMS, 48), jnp.bfloat16),
        pltpu.VMEM((slots, 3, 48, CELL_ATOMS), jnp.bfloat16),
        pltpu.VMEM((count * CELL_ATOMS, CELL_ATOMS), jnp.float32),
        pltpu.VMEM((count * CELL_ATOMS, CELL_ATOMS), jnp.float32),
        pltpu.VMEM((2 * count * CELL_ATOMS, CELL_ATOMS), jnp.bfloat16),
        pltpu.VMEM((2 * count * CELL_ATOMS, CELL_ATOMS), jnp.bfloat16),
    ]


def pair_sums(steps, units, base_of, finish, left_ref, right_ref, e0_ref, e1_ref, w0_ref, w1_ref):
    n = CELL_ATOMS

    def powers(step, e_ref):
        base = base_of(step)
        at = 0
        for _, center, others in units:
            for offset, delta in others:
                e_ref[at * n : (at + 1) * n] = jnp.dot(
                    left_ref[base + offset],
                    right_ref[base + center, 1 - delta],
                    preferred_element_type=jnp.float32,
                )
                at += 1

    def weights(e_ref, w_ref):
        at = 0
        for _, _, others in units:
            for number in range(len(others)):
                weight = jnp.exp2(e_ref[(at + number) * n : (at + number + 1) * n])
                high = weight.astype(jnp.bfloat16)
                low = (weight - high.astype(jnp.float32)).astype(jnp.bfloat16)
                place = 2 * at + number
                w_ref[place * n : (place + 1) * n] = high
                place += len(others)
                w_ref[place * n : (place + 1) * n] = low
            at += len(others)

    def sums(step, w_ref):
        base = base_of(step)
        at = 0
        for tag, _, others in units:
            rows = [right_ref[base + offset, delta + 1, 0:16] for offset, delta in others]
            total = jnp.dot(
                jnp.concatenate(rows + rows, axis=1),
                w_ref[2 * at * n : 2 * (at + len(others)) * n],
                preferred_element_type=jnp.float32,
            )
            finish(step, tag, total[:8] + total[8:])
            at += len(others)

    def clamp(step):
        return jnp.clip(step, 0, steps - 1)

    def pair(i, carry):
        step = 2 * i
        sums(clamp(step - 2), w0_ref)
        weights(e1_ref, w1_ref)
        powers(clamp(step), e0_ref)
        sums(clamp(step - 1), w1_ref)
        weights(e0_ref, w0_ref)
        powers(clamp(step + 1), e1_ref)
        return carry

    lax.fori_loop(0, (steps + 3) // 2, pair, 0)


def coefficient(center, sums):
    row = lax.broadcasted_iota(jnp.int32, sums.shape, 0)
    pulled = jnp.where(row == 0, sums + sums[7:8], sums)
    return (pair_strength / pair_range) * (center * sums[3:4] - pulled)


def place_loop(groups, span, one):
    def body(b, carry):
        for h in range(2):
            for u in range(span):
                cell = (h * groups + b) * span + u
                one(b, h * span + u, cell)
        return carry

    lax.fori_loop(0, groups, body, 0)


def lanes_of(cell):
    return pl.ds(pl.multiple_of(cell * LANES, LANES), LANES)


def send_kernel(q_ref, p_ref, f_ref, out_ref, *, groups, span):
    here = q_ref.shape[1]
    rows = here * 2 * span * 3
    quarter = 0.5 * time_step

    def one(b, tile, cell):
        lanes = lanes_of(cell)
        for c in range(3):
            row = b * 2 * rows + (tile * 3 + c) * here
            out_ref[pl.ds(row, here), :] = q_ref[c, :, lanes]
            out_ref[pl.ds(row + rows, here), :] = p_ref[c, :, lanes] + quarter * f_ref[c, :, lanes]

    place_loop(groups, span, one)


def columns_of(tiles):
    return [(t, c, slice((t * 3 + c) * LANES, (t * 3 + c + 1) * LANES)) for t in range(tiles) for c in range(3)]


def noise_kernel(drift_ref, mix_ref, aux_ref, noise_ref, first_ref, later_ref, rows_ref):
    beads = aux_ref.shape[0]
    size = AUX + 1
    tiles = aux_ref.shape[3] // LANES

    def copy(k, carry):
        for c in range(3):
            for t in range(tiles):
                rows_ref[c, t, pl.ds(k * AUX, AUX), :] = aux_ref[k, c, :, t * LANES : (t + 1) * LANES]
        return carry

    lax.fori_loop(0, beads, copy, 0)
    drift = drift_ref[...]
    mix = mix_ref[...]

    def mixed(s, a, c, inner):
        at = a * size
        total = mix[:, at : at + 1] * noise_ref[s, 0, c, :, inner]
        for b in range(1, size):
            total = total + mix[:, at + b : at + b + 1] * noise_ref[s, b, c, :, inner]
        return total

    for t, c, lanes in columns_of(tiles):
        inner = slice(t * LANES, (t + 1) * LANES)
        others = [rows_ref[c, t, pl.ds(b, beads, stride=AUX), :] for b in range(AUX)]
        news = []
        for a in range(size):
            total = mixed(0, a, c, inner)
            for b in range(AUX):
                total = total + drift[:, a * size + b + 1 : a * size + b + 2] * others[b]
            news.append(total)
        first_ref[:, lanes] = news[0]
        for a in range(size):
            total = mixed(1, a, c, inner)
            for b in range(1, size):
                total = total + drift[:, a * size + b : a * size + b + 1] * news[b]
            later_ref[a, :, lanes] = total


def twice(drift, a):
    size = AUX + 1
    total = drift[:, a * size + 1 : a * size + 2] * drift[:, size : size + 1]
    for b in range(2, size):
        total = total + drift[:, a * size + b : a * size + b + 1] * drift[:, b * size : b * size + 1]
    return total


def strided(ref, start, size, stride):
    return ref[pl.ds(start, size, stride=stride), :]


def turned(qm, p0, turn):
    cosine, sinc, wsin = turn[:, 0:1], turn[:, 1:2], turn[:, 2:3]
    return qm * cosine + sinc * p0, p0 * cosine - wsin * qm


def dot(a, b):
    return jnp.dot(a, b, precision=HIGHEST, preferred_element_type=jnp.float32)


def first_kernel(
    flag_ref, got_ref, pre_ref, gather_ref, basis_ref, turn_ref, drift_ref,
    own_ref, up0_ref, up1_ref, dn0_ref, dn1_ref, qn_ref, pn_ref, pm_ref, *, groups, span,
):
    beads = basis_ref.shape[0]
    here = beads // groups
    tiles = 2 * span
    rows = here * tiles * 3

    def gathered(which):
        columns = []
        for number in range(tiles * 3):
            parts = [
                strided(got_ref, which * rows + number * here + j, groups, 2 * rows) for j in range(here)
            ]
            columns.append(jnp.concatenate(parts, axis=0))
        return jnp.concatenate(columns, axis=1)

    gather = gather_ref[...]
    qm = dot(gather, gathered(0))
    pm = dot(gather, gathered(1))
    p0 = drift_ref[:, 0:1] * pm + pre_ref[...]
    qn, pn = turned(qm, p0, turn_ref[...])
    new = dot(basis_ref[...], qn)
    own_ref[...] = jnp.zeros_like(own_ref)
    value = {}
    for t, c, lanes in columns_of(tiles):
        value[t // span, t % span, c] = new[:, lanes]
        own_ref[t // span, t % span, pl.ds(c, beads, stride=8), :] = new[:, lanes]
    top = flag_ref[0] == groups - 1
    bottom = flag_ref[0] == 0
    for c in range(3):
        part = pl.ds(c * beads, beads)
        last0, last1 = value[0, span - 1, c], value[1, span - 1, c]
        up0_ref[part, :] = jnp.where(top, last1, last0)
        up1_ref[part, :] = jnp.where(top, last0, last1)
        dn0_ref[part, :] = jnp.where(bottom, value[1, 0, c], value[0, 0, c])
        dn1_ref[part, :] = jnp.where(bottom, value[0, 0, c], value[1, 0, c])
    qn_ref[...] = qn
    pn_ref[...] = pn
    pm_ref[...] = pm


def inner_kernel(own_ref, force_ref, *scratch, span, runs, units):
    beads = own_ref.shape[2] // 8
    left_ref, right_ref = scratch[:2]

    def tile(bead):
        return pl.ds(pl.multiple_of(bead * 8, 8), 8)

    def one(bead, carry):
        for h in range(2):
            for u in range(span):
                prepare(
                    own_ref[h, u, tile(bead), :], left_ref, right_ref,
                    (2 * bead + h) * (span + 2) + u + 1, True, (-1, 0, 1),
                )
        return carry

    lax.fori_loop(0, beads, one, 0)

    def finish(step, tag, sums):
        run, u = tag
        h, here = run % 2, tile(step * (runs // 2) + run // 2)
        force_ref[h, u, here, :] = coefficient(own_ref[h, u, here, :], sums)

    pair_sums(2 * beads // runs, units, lambda step: step * (runs * (span + 2)), finish, *scratch)


def outer_kernel(
    own_ref, part_ref, up0_ref, up1_ref, dn0_ref, dn1_ref, qn_ref, pn_ref, pm1_ref, later_ref,
    gather_ref, basis_ref, turn_ref, drift_ref,
    send_ref, pm_ref, halo_ref, force_ref, *scratch, groups, span, runs, units,
):
    beads = basis_ref.shape[0]
    here = beads // groups
    left_ref, right_ref = scratch[:2]
    halo_ref[...] = jnp.zeros_like(halo_ref)
    for number, ref in enumerate((up0_ref, up1_ref, dn0_ref, dn1_ref)):
        for c in range(3):
            halo_ref[number, pl.ds(c, beads, stride=8), :] = ref[pl.ds(c * beads, beads), :]

    def tile(bead):
        return pl.ds(pl.multiple_of(bead * 8, 8), 8)

    def one(bead, carry):
        at = tile(bead)
        for h in range(2):
            slot = (2 * bead + h) * (span + 2)
            prepare(halo_ref[h, at, :], left_ref, right_ref, slot, True, (-1,))
            prepare(halo_ref[2 + h, at, :], left_ref, right_ref, slot + span + 1, True, (1,))
            for u in sorted({0, span - 1}):
                shifts = ((1,) if u == 0 else ()) + ((-1,) if u == span - 1 else ())
                prepare(own_ref[h, u, at, :], left_ref, right_ref, slot + u + 1, False, shifts)
        return carry

    lax.fori_loop(0, beads, one, 0)
    force_ref[...] = part_ref[...]

    def finish(step, tag, sums):
        run, u = tag
        h, at = run % 2, tile(step * (runs // 2) + run // 2)
        force_ref[h, u, at, :] = part_ref[h, u, at, :] + coefficient(own_ref[h, u, at, :], sums)

    pair_sums(2 * beads // runs, units, lambda step: step * (runs * (span + 2)), finish, *scratch)

    force = jnp.concatenate(
        [strided(force_ref.at[t // span, t % span], c, beads, 8) for t, c, _ in columns_of(2 * span)], axis=1
    )
    pm = pn_ref[...] + time_step * dot(gather_ref[...], force)
    drift = drift_ref[...]
    p0 = drift[:, 0:1] * pm + (twice(drift, 0) * pm1_ref[...] + later_ref[...])
    qn, pn = turned(qn_ref[...], p0, turn_ref[...])
    count = 6 * span
    for which, modes in enumerate((qn, pn)):
        new = dot(basis_ref[...], modes)
        for number in range(count):
            for j in range(here):
                place = pl.ds((which * count + number) * here + j, groups, stride=2 * count * here)
                send_ref[place, :] = new[j * groups : (j + 1) * groups, number * LANES : (number + 1) * LANES]
    pm_ref[...] = pm


def rest_kernel(pm1_ref, pm_ref, later_ref, drift_ref, out_ref, rows_ref, *, span):
    beads = pm_ref.shape[0]
    size = AUX + 1
    drift = drift_ref[...]
    again = [twice(drift, a) for a in range(1, size)]
    for t, c, lanes in columns_of(2 * span):
        pm1 = pm1_ref[:, lanes]
        pm = pm_ref[:, lanes]
        for a in range(1, size):
            rows_ref[c, t, pl.ds(a - 1, beads, stride=AUX), :] = drift[:, a * size : a * size + 1] * pm + (
                again[a - 1] * pm1 + later_ref[a, :, lanes]
            )

    def copy(k, carry):
        for c in range(3):
            for t in range(2 * span):
                out_ref[k, c, :, t * LANES : (t + 1) * LANES] = rows_ref[c, t, pl.ds(k * AUX, AUX), :]
        return carry

    lax.fori_loop(0, beads, copy, 0)


def bead_kernel(
    got_ref, before_ref, after_ref, q_ref, p_ref, f_ref, x_ref, force_ref, *scratch, groups, span, block, units
):
    here = q_ref.shape[1]
    half = 0.5 * time_step
    rows = 6 * span * here
    cells = q_ref.shape[2] // LANES
    left_ref, right_ref = scratch[:2]
    x_ref[...] = jnp.zeros_like(x_ref)
    for j in range(here):
        x_ref[j * (cells + 2), 0:3] = strided(before_ref, j, 3, here)
        x_ref[(j + 1) * (cells + 2) - 1, 0:3] = strided(after_ref, j, 3, here)

    def place(b, tile, cell):
        row = b * 2 * rows + tile * 3 * here
        for c in range(3):
            q_ref[c, :, lanes_of(cell)] = got_ref[pl.ds(row + c * here, here), :]
        for j in range(here):
            x_ref[j * (cells + 2) + cell + 1, 0:3] = got_ref[pl.ds(row + j, 3, stride=here), :]

    place_loop(groups, span, place)
    slots = here * (cells + 2)
    group = math.gcd(slots, 4)

    def one(number, carry):
        for k in range(group):
            slot = number * group + k
            prepare(x_ref[slot], left_ref, right_ref, slot, True, (-1, 0, 1))
        return carry

    lax.fori_loop(0, slots // group, one, 0)
    per_bead = cells // block

    def base_of(step):
        return (step // per_bead) * (cells + 2) + (step % per_bead) * block

    def finish(step, u, sums):
        at = pl.multiple_of((step * block + u) * 8, 8)
        force_ref[pl.ds(at, 8), :] = coefficient(x_ref[base_of(step) + 1 + u], sums)

    pair_sums(here * per_bead, units, base_of, finish, *scratch)

    def out(b, tile, cell):
        row = b * 2 * rows + rows + tile * 3 * here
        for c in range(3):
            force = strided(force_ref, cell * 8 + c, here, cells * 8)
            f_ref[c, :, lanes_of(cell)] = force
            p_ref[c, :, lanes_of(cell)] = got_ref[pl.ds(row + c * here, here), :] + half * force

    place_loop(groups, span, out)


def on_device(positions, momenta, forces, gle_drift, gle_noise_mix, aux_momenta, noise):
    here, _, atoms_here = positions.shape
    beads = gle_drift.shape[0]
    groups = lax.axis_size("bead")
    spaces = lax.axis_size("space")
    span = atoms_here // (2 * groups * CELL_ATOMS)
    cells = atoms_here // CELL_ATOMS
    columns = 2 * span * 3
    width = columns * LANES
    size = AUX + 1
    basis, turn = mode_tables(beads)
    order = np.array([b * here + j for j in range(here) for b in range(groups)])
    gather = jnp.asarray(np.ascontiguousarray(basis[order].T))
    basis = jnp.asarray(np.ascontiguousarray(basis[order]))
    turn = jnp.asarray(turn)
    drift = gle_drift.reshape(beads, size * size)
    mix = gle_noise_mix.reshape(beads, size * size)
    me = lax.axis_index("bead").astype(jnp.int32).reshape(1)
    by_coord = functools.partial(jnp.transpose, axes=(1, 0, 2))
    grid = f32(3, here, atoms_here)

    def exchanged(block):
        return lax.all_to_all(block, "bead", split_axis=0, concat_axis=0, tiled=True)

    send = call(
        functools.partial(send_kernel, groups=groups, span=span),
        f32(groups * 2 * here * columns, LANES),
        [VMEM_SPEC] * 3,
    )(by_coord(positions), by_coord(momenta), by_coord(forces))
    got = exchanged(send)
    rows = pltpu.VMEM((3, 2 * span, beads * AUX, LANES), jnp.float32)
    first, later = call(
        noise_kernel,
        [f32(beads, width), f32(size, beads, width)],
        [VMEM_SPEC] * 4,
        scratch_shapes=[rows],
    )(drift, mix, jnp.transpose(aux_momenta, (0, 2, 1, 3)), jnp.transpose(noise, (0, 2, 3, 1, 4)))

    halo = f32(beads * 3, LANES)
    state = f32(beads, width)
    own, up0, up1, dn0, dn1, qn, pn, pm = call(
        functools.partial(first_kernel, groups=groups, span=span),
        [f32(2, span, beads * 8, LANES), halo, halo, halo, halo, state, state, state],
        [SMEM_SPEC] + [VMEM_SPEC] * 6,
    )(me, got, first, gather, basis, turn, drift)

    def shifted(block, step, wrap):
        route = []
        for b in range(groups):
            for s in range(spaces):
                to_b, to_s = b + step, s
                if not 0 <= to_b < groups:
                    to_b, to_s = to_b % groups, (s + wrap) % spaces
                route.append((b * spaces + s, to_b * spaces + to_s))
        return lax.ppermute(block, ("bead", "space"), route)

    up0 = shifted(up0, 1, 1)
    up1 = shifted(up1, 1, 0)
    dn0 = shifted(dn0, -1, 0)
    dn1 = shifted(dn1, -1, -1)

    slots = 2 * beads * (span + 2)
    inside, outside = [], []
    inside_runs, outside_runs = math.gcd(2 * beads, 4), math.gcd(2 * beads, 8)
    for runs, units, near in ((inside_runs, inside, range(span)), (outside_runs, outside, (-1, span))):
        for run in range(runs):
            for u in range(span):
                at = run * (span + 2) + 1
                others = [(at + v, v - u) for v in near if abs(v - u) <= 1]
                if others:
                    units.append(((run, u), at + u, others))
    part = call(
        functools.partial(inner_kernel, span=span, runs=inside_runs, units=inside),
        f32(2, span, beads * 8, LANES),
        [VMEM_SPEC],
        scratch_shapes=pair_scratch(slots, inside),
    )(own)
    send, pm2 = call(
        functools.partial(outer_kernel, groups=groups, span=span, runs=outside_runs, units=outside),
        [f32(2 * beads * columns, LANES), state],
        [VMEM_SPEC] * 14,
        scratch_shapes=[
            pltpu.VMEM((4, beads * 8, LANES), jnp.float32),
            pltpu.VMEM((2, span, beads * 8, LANES), jnp.float32),
        ]
        + pair_scratch(slots, outside),
    )(own, part, up0, up1, dn0, dn1, qn, pn, pm, later[0], gather, basis, turn, drift)
    got = exchanged(send)
    aux_out = call(
        functools.partial(rest_kernel, span=span),
        f32(beads, 3, AUX, aux_momenta.shape[3]),
        [VMEM_SPEC] * 4,
        scratch_shapes=[rows],
    )(pm, pm2, later, drift)

    head = got[: 3 * here]
    end = (2 * groups - 1) * here * columns
    tail = got[end - 3 * here : end]
    before = lax.ppermute(tail, "space", [(s, (s + 1) % spaces) for s in range(spaces)])
    after = lax.ppermute(head, "space", [(s, (s - 1) % spaces) for s in range(spaces)])
    block = math.gcd(cells, 4)
    around = [(u, u + 1, [(u, -1), (u + 1, 0), (u + 2, 1)]) for u in range(block)]
    new_q, new_p, new_f = call(
        functools.partial(bead_kernel, groups=groups, span=span, block=block, units=around),
        [grid] * 3,
        [VMEM_SPEC] * 3,
        scratch_shapes=[
            pltpu.VMEM((here * (cells + 2), 8, LANES), jnp.float32),
            pltpu.VMEM((here * cells * 8, LANES), jnp.float32),
        ]
        + pair_scratch(here * (cells + 2), around),
    )(got, before, after)
    return by_coord(new_q), by_coord(new_p), by_coord(new_f), jnp.transpose(aux_out, (0, 2, 1, 3))


def solution(mesh):
    in_specs = (
        P("bead", None, "space"),
        P("bead", None, "space"),
        P("bead", None, "space"),
        P(),
        P(),
        P(None, None, None, ("space", "bead")),
        P(None, None, None, None, ("space", "bead")),
    )
    out_specs = (
        P("bead", None, "space"),
        P("bead", None, "space"),
        P("bead", None, "space"),
        P(None, None, None, ("space", "bead")),
    )
    return jax.shard_map(
        on_device, mesh=mesh, in_specs=in_specs, out_specs=out_specs, check_vma=False
    )
```

```python
import functools
import math

import jax
import jax.numpy as jnp
import ml_dtypes
import numpy as np
from jax import lax
from jax.experimental import pallas as pl
from jax.experimental.pallas import tpu as pltpu
from jax.sharding import PartitionSpec as P

CELL_ATOMS = 128
AUX = 4
STEPS = 2

time_step = 0.5
cycle_freq = 1.5
cell_length = 2.0
pair_strength = 0.1
pair_range = 1.0

LANES = 128
LOG2E = math.log2(math.e)
HIGHEST = lax.Precision.HIGHEST
VMEM_SPEC = pl.BlockSpec(memory_space=pltpu.VMEM)
SMEM_SPEC = pl.BlockSpec(memory_space=pltpu.SMEM)


def call(kernel, out_shape, in_specs=None, scratch_shapes=(), **kwargs):
    many = isinstance(out_shape, (list, tuple))
    return pl.pallas_call(
        kernel,
        out_shape=out_shape,
        in_specs=in_specs,
        out_specs=[VMEM_SPEC] * len(out_shape) if many else VMEM_SPEC,
        scratch_shapes=scratch_shapes,
        compiler_params=pltpu.CompilerParams(vmem_limit_bytes=56 * 1024 * 1024),
        **kwargs,
    )


def f32(*shape):
    return jax.ShapeDtypeStruct(shape, jnp.float32)


def mode_tables(beads):
    j = np.arange(beads, dtype=np.float64)[:, None]
    k = np.arange(beads)[None, :]
    phase = 2.0 * np.pi * j * k / beads
    basis = np.where(
        k == 0,
        np.sqrt(1.0 / beads),
        np.where(
            k < beads // 2,
            np.sqrt(2.0 / beads) * np.cos(phase),
            np.where(
                k == beads // 2, np.sqrt(1.0 / beads) * np.cos(phase), np.sqrt(2.0 / beads) * np.sin(phase)
            ),
        ),
    )
    freq = 2.0 * cycle_freq * np.sin(np.pi * np.arange(beads) / beads)
    cosine = np.cos(time_step * freq)
    safe = np.where(np.arange(beads) == 0, 1.0, freq)
    sinc = np.where(np.arange(beads) == 0, time_step, np.sin(time_step * freq) / safe)
    wsin = freq * np.sin(time_step * freq)
    turn = np.stack([cosine, sinc, wsin], axis=1)
    return basis.astype(np.float32), turn.astype(np.float32)


def split3(value):
    first = value.astype(jnp.bfloat16).astype(jnp.float32)
    rest = value - first
    second = rest.astype(jnp.bfloat16).astype(jnp.float32)
    third = rest - second
    return first, second, third


def prepare(coords, left_ref, right_ref, slot, want_left, shifts):
    row = lax.broadcasted_iota(jnp.int32, coords.shape, 0)
    scale = LOG2E / pair_range
    square = (0.5 * scale) * jnp.sum(coords * coords, axis=0, keepdims=True)
    along = coords[0:1]
    if want_left:
        x = jnp.where(row > 3, 1.0, coords * scale)
        x = jnp.where(row == 3, -square, x)
        x = jnp.where(row == 7, along * scale, x)
        a1, a2, a3 = split3(x)
        left = jnp.concatenate([a1, a1, a2, a2, a1, a3], axis=0)
        left_ref[slot] = jnp.transpose(left).astype(jnp.bfloat16)
    shift = (row - 5).astype(jnp.float32) * cell_length
    x = jnp.where(row > 3, -square - scale * (shift * along + 0.5 * shift * shift), coords)
    x = jnp.where(row == 3, 1.0, x)
    b1, b2, b3 = split3(x)
    for delta in shifts:
        keep = (row <= 3) | (row == 5 + delta)
        c1 = jnp.where(keep, b1, jnp.where(row == 7, delta * cell_length, 0.0))
        c2 = jnp.where(keep, b2, 0.0)
        c3 = jnp.where(keep, b3, 0.0)
        right_ref[slot, delta + 1] = jnp.concatenate([c1, c2, c1, c2, c3, c1], axis=0).astype(jnp.bfloat16)


def pair_scratch(slots, units):
    count = sum(len(others) for _, _, others in units)
    return [
        pltpu.VMEM((slots, CELL_ATOMS, 48), jnp.bfloat16),
        pltpu.VMEM((slots, 3, 48, CELL_ATOMS), jnp.bfloat16),
        pltpu.VMEM((count * CELL_ATOMS, CELL_ATOMS), jnp.float32),
        pltpu.VMEM((count * CELL_ATOMS, CELL_ATOMS), jnp.float32),
        pltpu.VMEM((2 * count * CELL_ATOMS, CELL_ATOMS), jnp.bfloat16),
        pltpu.VMEM((2 * count * CELL_ATOMS, CELL_ATOMS), jnp.bfloat16),
    ]


def pair_sums(steps, units, base_of, finish, left_ref, right_ref, e0_ref, e1_ref, w0_ref, w1_ref):
    n = CELL_ATOMS
    starts = [sum(len(others) for _, _, others in units[:k]) for k in range(len(units))]

    def powers(k, step, e_ref):
        base = base_of(step)
        _, center, others = units[k]
        for number, (offset, delta) in enumerate(others):
            at = starts[k] + number
            e_ref[at * n : (at + 1) * n] = jnp.dot(
                left_ref[base + offset],
                right_ref[base + center, 1 - delta],
                preferred_element_type=jnp.float32,
            )

    def weights(k, e_ref, w_ref):
        count = len(units[k][2])
        for number in range(count):
            at = starts[k] + number
            weight = jnp.exp2(e_ref[at * n : (at + 1) * n])
            high = weight.astype(jnp.bfloat16)
            low = (weight - high.astype(jnp.float32)).astype(jnp.bfloat16)
            place = 2 * starts[k] + number
            w_ref[place * n : (place + 1) * n] = high
            place += count
            w_ref[place * n : (place + 1) * n] = low

    def sums(k, step, w_ref):
        base = base_of(step)
        tag, _, others = units[k]
        rows = [right_ref[base + offset, delta + 1, 0:16] for offset, delta in others]
        at = starts[k]
        total = jnp.dot(
            jnp.concatenate(rows + rows, axis=1),
            w_ref[2 * at * n : 2 * (at + len(others)) * n],
            preferred_element_type=jnp.float32,
        )
        finish(step, tag, total[:8] + total[8:])

    def clamp(step):
        return jnp.clip(step, 0, steps - 1)

    def pair(i, carry):
        step = 2 * i
        for first, e_new, e_old, w_new, w_old in (
            (step, e0_ref, e1_ref, w1_ref, w0_ref),
            (step + 1, e1_ref, e0_ref, w0_ref, w1_ref),
        ):
            for k in range(len(units)):
                powers(k, clamp(first), e_new)
                weights(k, e_old, w_new)
                sums(k, clamp(first - 2), w_old)
        return carry

    lax.fori_loop(0, (steps + 3) // 2, pair, 0)


def coefficient(center, sums):
    row = lax.broadcasted_iota(jnp.int32, sums.shape, 0)
    pulled = jnp.where(row == 0, sums + sums[7:8], sums)
    return (pair_strength / pair_range) * (center * sums[3:4] - pulled)


def place_loop(groups, span, one):
    def body(b, carry):
        for h in range(2):
            for u in range(span):
                cell = (h * groups + b) * span + u
                one(b, h * span + u, cell)
        return carry

    lax.fori_loop(0, groups, body, 0)


def lanes_of(cell):
    return pl.ds(pl.multiple_of(cell * LANES, LANES), LANES)


def send_kernel(q_ref, p_ref, f_ref, out_ref, *, groups, span):
    here = q_ref.shape[1]
    rows = here * 2 * span * 3
    quarter = 0.5 * time_step

    def one(b, tile, cell):
        lanes = lanes_of(cell)
        for c in range(3):
            row = b * 2 * rows + (tile * 3 + c) * here
            out_ref[pl.ds(row, here), :] = q_ref[c, :, lanes]
            out_ref[pl.ds(row + rows, here), :] = p_ref[c, :, lanes] + quarter * f_ref[c, :, lanes]

    place_loop(groups, span, one)


def columns_of(tiles):
    return [(t, c, slice((t * 3 + c) * LANES, (t * 3 + c + 1) * LANES)) for t in range(tiles) for c in range(3)]


def noise_kernel(drift_ref, mix_ref, aux_ref, noise_ref, first_ref, later0_ref, later_ref, rows_ref):
    beads = aux_ref.shape[0]
    size = AUX + 1
    tiles = aux_ref.shape[3] // LANES

    def copy(k, carry):
        for c in range(3):
            for t in range(tiles):
                rows_ref[c, t, pl.ds(k * AUX, AUX), :] = aux_ref[k, c, :, t * LANES : (t + 1) * LANES]
        return carry

    lax.fori_loop(0, beads, copy, 0)
    drift = drift_ref[...]
    mix = mix_ref[...]

    def mixed(s, a, c, inner):
        at = a * size
        total = mix[:, at : at + 1] * noise_ref[s, 0, c, :, inner]
        for b in range(1, size):
            total = total + mix[:, at + b : at + b + 1] * noise_ref[s, b, c, :, inner]
        return total

    for t, c, lanes in columns_of(tiles):
        inner = slice(t * LANES, (t + 1) * LANES)
        others = [rows_ref[c, t, pl.ds(b, beads, stride=AUX), :] for b in range(AUX)]
        news = []
        for a in range(size):
            total = mixed(0, a, c, inner)
            for b in range(AUX):
                total = total + drift[:, a * size + b + 1 : a * size + b + 2] * others[b]
            news.append(total)
        first_ref[:, lanes] = news[0]
        for a in range(size):
            total = mixed(1, a, c, inner)
            for b in range(1, size):
                total = total + drift[:, a * size + b : a * size + b + 1] * news[b]
            if a == 0:
                later0_ref[:, lanes] = total
            else:
                later_ref[a - 1, :, lanes] = total


def twice(drift, a):
    size = AUX + 1
    total = drift[:, a * size + 1 : a * size + 2] * drift[:, size : size + 1]
    for b in range(2, size):
        total = total + drift[:, a * size + b : a * size + b + 1] * drift[:, b * size : b * size + 1]
    return total


def strided(ref, start, size, stride):
    return ref[pl.ds(start, size, stride=stride), :]


def turned(qm, p0, turn):
    cosine, sinc, wsin = turn[:, 0:1], turn[:, 1:2], turn[:, 2:3]
    return qm * cosine + sinc * p0, p0 * cosine - wsin * qm


def dot(a, b):
    return jnp.dot(a, b, precision=HIGHEST, preferred_element_type=jnp.float32)


def first_kernel(
    flag_ref, got_ref, pre_ref, gather_ref, basis_ref, turn_ref, drift_ref,
    own_ref, up0_ref, up1_ref, dn0_ref, dn1_ref, qn_ref, pn_ref, pm_ref, *, groups, span,
):
    beads = basis_ref.shape[0]
    here = beads // groups
    tiles = 2 * span
    rows = here * tiles * 3

    def gathered(which):
        columns = []
        for number in range(tiles * 3):
            parts = [
                strided(got_ref, which * rows + number * here + j, groups, 2 * rows) for j in range(here)
            ]
            columns.append(jnp.concatenate(parts, axis=0))
        return jnp.concatenate(columns, axis=1)

    gather = gather_ref[...]
    qm = dot(gather, gathered(0))
    pm = dot(gather, gathered(1))
    p0 = drift_ref[:, 0:1] * pm + pre_ref[...]
    qn, pn = turned(qm, p0, turn_ref[...])
    new = dot(basis_ref[...], qn)
    own_ref[...] = jnp.zeros_like(own_ref)
    value = {}
    for t, c, lanes in columns_of(tiles):
        value[t // span, t % span, c] = new[:, lanes]
        own_ref[t // span, t % span, pl.ds(c, beads, stride=8), :] = new[:, lanes]
    top = flag_ref[0] == groups - 1
    bottom = flag_ref[0] == 0
    for c in range(3):
        part = pl.ds(c * beads, beads)
        last0, last1 = value[0, span - 1, c], value[1, span - 1, c]
        up0_ref[part, :] = jnp.where(top, last1, last0)
        up1_ref[part, :] = jnp.where(top, last0, last1)
        dn0_ref[part, :] = jnp.where(bottom, value[1, 0, c], value[0, 0, c])
        dn1_ref[part, :] = jnp.where(bottom, value[0, 0, c], value[1, 0, c])
    qn_ref[...] = qn
    pn_ref[...] = pn
    pm_ref[...] = pm


def inner_kernel(own_ref, force_ref, *scratch, span, runs, units):
    beads = own_ref.shape[2] // 8
    left_ref, right_ref = scratch[:2]

    def tile(bead):
        return pl.ds(pl.multiple_of(bead * 8, 8), 8)

    def one(bead, carry):
        for h in range(2):
            for u in range(span):
                prepare(
                    own_ref[h, u, tile(bead), :], left_ref, right_ref,
                    (2 * bead + h) * (span + 2) + u + 1, True, (-1, 0, 1),
                )
        return carry

    lax.fori_loop(0, beads, one, 0)

    def finish(step, tag, sums):
        run, u = tag
        h, here = run % 2, tile(step * (runs // 2) + run // 2)
        force_ref[h, u, here, :] = coefficient(own_ref[h, u, here, :], sums)

    pair_sums(2 * beads // runs, units, lambda step: step * (runs * (span + 2)), finish, *scratch)


def outer_kernel(
    own_ref, part_ref, up0_ref, up1_ref, dn0_ref, dn1_ref, qn_ref, pn_ref, pm1_ref, later_ref,
    gather_ref, basis_ref, turn_ref, drift_ref,
    send_ref, pm_ref, halo_ref, force_ref, *scratch, groups, span, runs, units,
):
    beads = basis_ref.shape[0]
    here = beads // groups
    left_ref, right_ref = scratch[:2]
    halo_ref[...] = jnp.zeros_like(halo_ref)
    for number, ref in enumerate((up0_ref, up1_ref, dn0_ref, dn1_ref)):
        for c in range(3):
            halo_ref[number, pl.ds(c, beads, stride=8), :] = ref[pl.ds(c * beads, beads), :]

    def tile(bead):
        return pl.ds(pl.multiple_of(bead * 8, 8), 8)

    def one(bead, carry):
        at = tile(bead)
        for h in range(2):
            slot = (2 * bead + h) * (span + 2)
            prepare(halo_ref[h, at, :], left_ref, right_ref, slot, True, (-1,))
            prepare(halo_ref[2 + h, at, :], left_ref, right_ref, slot + span + 1, True, (1,))
            for u in sorted({0, span - 1}):
                shifts = ((1,) if u == 0 else ()) + ((-1,) if u == span - 1 else ())
                prepare(own_ref[h, u, at, :], left_ref, right_ref, slot + u + 1, False, shifts)
        return carry

    lax.fori_loop(0, beads, one, 0)
    force_ref[...] = part_ref[...]

    def finish(step, tag, sums):
        run, u = tag
        h, at = run % 2, tile(step * (runs // 2) + run // 2)
        force_ref[h, u, at, :] = part_ref[h, u, at, :] + coefficient(own_ref[h, u, at, :], sums)

    pair_sums(2 * beads // runs, units, lambda step: step * (runs * (span + 2)), finish, *scratch)

    force = jnp.concatenate(
        [strided(force_ref.at[t // span, t % span], c, beads, 8) for t, c, _ in columns_of(2 * span)], axis=1
    )
    pm = pn_ref[...] + time_step * dot(gather_ref[...], force)
    drift = drift_ref[...]
    p0 = drift[:, 0:1] * pm + (twice(drift, 0) * pm1_ref[...] + later_ref[...])
    qn, pn = turned(qn_ref[...], p0, turn_ref[...])
    count = 6 * span
    for which, modes in enumerate((qn, pn)):
        new = dot(basis_ref[...], modes)
        for number in range(count):
            for j in range(here):
                place = pl.ds((which * count + number) * here + j, groups, stride=2 * count * here)
                send_ref[place, :] = new[j * groups : (j + 1) * groups, number * LANES : (number + 1) * LANES]
    pm_ref[...] = pm


def rest_kernel(pm1_ref, pm_ref, later_ref, drift_ref, out_ref, rows_ref, *, span):
    beads = pm_ref.shape[0]
    size = AUX + 1
    drift = drift_ref[...]
    again = [twice(drift, a) for a in range(1, size)]
    for t, c, lanes in columns_of(2 * span):
        pm1 = pm1_ref[:, lanes]
        pm = pm_ref[:, lanes]
        for a in range(1, size):
            rows_ref[c, t, pl.ds(a - 1, beads, stride=AUX), :] = drift[:, a * size : a * size + 1] * pm + (
                again[a - 1] * pm1 + later_ref[a - 1, :, lanes]
            )

    def copy(k, carry):
        for c in range(3):
            for t in range(2 * span):
                out_ref[k, c, :, t * LANES : (t + 1) * LANES] = rows_ref[c, t, pl.ds(k * AUX, AUX), :]
        return carry

    lax.fori_loop(0, beads, copy, 0)


def bead_kernel(
    got_ref, before_ref, after_ref, q_ref, p_ref, f_ref, x_ref, force_ref, *scratch, groups, span, block, units
):
    here = q_ref.shape[1]
    half = 0.5 * time_step
    rows = 6 * span * here
    cells = q_ref.shape[2] // LANES
    left_ref, right_ref = scratch[:2]
    x_ref[...] = jnp.zeros_like(x_ref)
    for j in range(here):
        x_ref[j * (cells + 2), 0:3] = strided(before_ref, j, 3, here)
        x_ref[(j + 1) * (cells + 2) - 1, 0:3] = strided(after_ref, j, 3, here)

    def place(b, tile, cell):
        row = b * 2 * rows + tile * 3 * here
        for c in range(3):
            q_ref[c, :, lanes_of(cell)] = got_ref[pl.ds(row + c * here, here), :]
        for j in range(here):
            x_ref[j * (cells + 2) + cell + 1, 0:3] = got_ref[pl.ds(row + j, 3, stride=here), :]

    place_loop(groups, span, place)
    slots = here * (cells + 2)
    group = math.gcd(slots, 4)

    def one(number, carry):
        for k in range(group):
            slot = number * group + k
            prepare(x_ref[slot], left_ref, right_ref, slot, True, (-1, 0, 1))
        return carry

    lax.fori_loop(0, slots // group, one, 0)
    per_bead = cells // block

    def base_of(step):
        return (step // per_bead) * (cells + 2) + (step % per_bead) * block

    def finish(step, u, sums):
        at = pl.multiple_of((step * block + u) * 8, 8)
        force_ref[pl.ds(at, 8), :] = coefficient(x_ref[base_of(step) + 1 + u], sums)

    pair_sums(here * per_bead, units, base_of, finish, *scratch)

    def out(b, tile, cell):
        row = b * 2 * rows + rows + tile * 3 * here
        for c in range(3):
            force = strided(force_ref, cell * 8 + c, here, cells * 8)
            f_ref[c, :, lanes_of(cell)] = force
            p_ref[c, :, lanes_of(cell)] = got_ref[pl.ds(row + c * here, here), :] + half * force

    place_loop(groups, span, out)


def on_device(positions, momenta, forces, gle_drift, gle_noise_mix, aux_momenta, noise):
    here, _, atoms_here = positions.shape
    beads = gle_drift.shape[0]
    groups = lax.axis_size("bead")
    spaces = lax.axis_size("space")
    span = atoms_here // (2 * groups * CELL_ATOMS)
    cells = atoms_here // CELL_ATOMS
    columns = 2 * span * 3
    width = columns * LANES
    size = AUX + 1
    basis, turn = mode_tables(beads)
    order = np.array([b * here + j for j in range(here) for b in range(groups)])
    gather = jnp.asarray(np.ascontiguousarray(basis[order].T))
    basis = jnp.asarray(np.ascontiguousarray(basis[order]))
    turn = jnp.asarray(turn)
    drift = gle_drift.reshape(beads, size * size)
    mix = gle_noise_mix.reshape(beads, size * size)
    me = lax.axis_index("bead").astype(jnp.int32).reshape(1)
    by_coord = functools.partial(jnp.transpose, axes=(1, 0, 2))
    grid = f32(3, here, atoms_here)

    def exchanged(block):
        return lax.all_to_all(block, "bead", split_axis=0, concat_axis=0, tiled=True)

    send = call(
        functools.partial(send_kernel, groups=groups, span=span),
        f32(groups * 2 * here * columns, LANES),
        [VMEM_SPEC] * 3,
    )(by_coord(positions), by_coord(momenta), by_coord(forces))
    got = exchanged(send)
    rows = pltpu.VMEM((3, 2 * span, beads * AUX, LANES), jnp.float32)
    first, later0, later = call(
        noise_kernel,
        [f32(beads, width), f32(beads, width), f32(AUX, beads, width)],
        [VMEM_SPEC] * 4,
        scratch_shapes=[rows],
    )(drift, mix, jnp.transpose(aux_momenta, (0, 2, 1, 3)), jnp.transpose(noise, (0, 2, 3, 1, 4)))

    halo = f32(beads * 3, LANES)
    state = f32(beads, width)
    own, up0, up1, dn0, dn1, qn, pn, pm = call(
        functools.partial(first_kernel, groups=groups, span=span),
        [f32(2, span, beads * 8, LANES), halo, halo, halo, halo, state, state, state],
        [SMEM_SPEC] + [VMEM_SPEC] * 6,
    )(me, got, first, gather, basis, turn, drift)

    def shifted(block, step, wrap):
        route = []
        for b in range(groups):
            for s in range(spaces):
                to_b, to_s = b + step, s
                if not 0 <= to_b < groups:
                    to_b, to_s = to_b % groups, (s + wrap) % spaces
                route.append((b * spaces + s, to_b * spaces + to_s))
        return lax.ppermute(block, ("bead", "space"), route)

    up0 = shifted(up0, 1, 1)
    up1 = shifted(up1, 1, 0)
    dn0 = shifted(dn0, -1, 0)
    dn1 = shifted(dn1, -1, -1)

    slots = 2 * beads * (span + 2)
    inside, outside = [], []
    inside_runs, outside_runs = math.gcd(2 * beads, 8), math.gcd(2 * beads, 8)
    for runs, units, near in ((inside_runs, inside, range(span)), (outside_runs, outside, (-1, span))):
        for run in range(runs):
            for u in range(span):
                at = run * (span + 2) + 1
                others = [(at + v, v - u) for v in near if abs(v - u) <= 1]
                if others:
                    units.append(((run, u), at + u, others))
    part = call(
        functools.partial(inner_kernel, span=span, runs=inside_runs, units=inside),
        f32(2, span, beads * 8, LANES),
        [VMEM_SPEC],
        scratch_shapes=pair_scratch(slots, inside),
    )(own)
    send, pm2 = call(
        functools.partial(outer_kernel, groups=groups, span=span, runs=outside_runs, units=outside),
        [f32(2 * beads * columns, LANES), state],
        [VMEM_SPEC] * 14,
        scratch_shapes=[
            pltpu.VMEM((4, beads * 8, LANES), jnp.float32),
            pltpu.VMEM((2, span, beads * 8, LANES), jnp.float32),
        ]
        + pair_scratch(slots, outside),
    )(own, part, up0, up1, dn0, dn1, qn, pn, pm, later0, gather, basis, turn, drift)
    got = exchanged(send)
    aux_out = call(
        functools.partial(rest_kernel, span=span),
        f32(beads, 3, AUX, aux_momenta.shape[3]),
        [VMEM_SPEC] * 4,
        scratch_shapes=[rows],
    )(pm, pm2, later, drift)
    got, aux_out = lax.optimization_barrier((got, aux_out))

    head = got[: 3 * here]
    end = (2 * groups - 1) * here * columns
    tail = got[end - 3 * here : end]
    before = lax.ppermute(tail, "space", [(s, (s + 1) % spaces) for s in range(spaces)])
    after = lax.ppermute(head, "space", [(s, (s - 1) % spaces) for s in range(spaces)])
    block = math.gcd(cells, 8)
    around = [(u, u + 1, [(u, -1), (u + 1, 0), (u + 2, 1)]) for u in range(block)]
    new_q, new_p, new_f = call(
        functools.partial(bead_kernel, groups=groups, span=span, block=block, units=around),
        [grid] * 3,
        [VMEM_SPEC] * 3,
        scratch_shapes=[
            pltpu.VMEM((here * (cells + 2), 8, LANES), jnp.float32),
            pltpu.VMEM((here * cells * 8, LANES), jnp.float32),
        ]
        + pair_scratch(here * (cells + 2), around),
    )(got, before, after)
    return by_coord(new_q), by_coord(new_p), by_coord(new_f), jnp.transpose(aux_out, (0, 2, 1, 3))


def solution(mesh):
    in_specs = (
        P("bead", None, "space"),
        P("bead", None, "space"),
        P("bead", None, "space"),
        P(),
        P(),
        P(None, None, None, ("space", "bead")),
        P(None, None, None, None, ("space", "bead")),
    )
    out_specs = (
        P("bead", None, "space"),
        P("bead", None, "space"),
        P("bead", None, "space"),
        P(None, None, None, ("space", "bead")),
    )
    return jax.shard_map(
        on_device, mesh=mesh, in_specs=in_specs, out_specs=out_specs, check_vma=False
    )
```
